512 devices in a mesh: dp: 64 (over y_lo, z, core), tensor: 8 (over x, y_hi).
Axes of the slice: x: 4, y: 8 (y_hi: 2, y_lo: 4; y = y_hi * 4 + y_lo), z: 8, core: 2. Of those that a mesh axis runs over, the one named last changes fastest.
Arguments:
- cotangent: bfloat16 [65536, 3072], P(('dp', 'tensor')), may hold values from -6 to 6
- context: bfloat16 [65536, 3072], P('dp', 'tensor'), may hold values from -6 to 6
- master: float32 [3072, 3072], P('dp', 'tensor'), may hold values from -0.109375 to 0.109375
- first_moment: float32 [3072, 3072], P('dp', 'tensor'), may hold values from -0.0234375 to 0.0234375
- second_moment: float32 [3072, 3072], P('dp', 'tensor'), as said below
Outputs:
- d_context: bfloat16 [65536, 3072], P('dp', 'tensor')
- new_master: float32 [3072, 3072], P('dp', 'tensor')
- new_first: float32 [3072, 3072], P('dp', 'tensor')
- new_second: float32 [3072, 3072], P('dp', 'tensor')
- new_weights: bfloat16 [3072, 3072], P(None, 'tensor')
The draws below stay inside these ranges and needn't reach their ends.
Inputs may be any that keep to these rules, and one draw needn't show every extreme that they name: second_moment is positive.
All inputs are finite; a program needn't handle non-finite values.
Results may differ from the reference program's by a relative error of at most 0.0049.
Values may be sent and summed in bfloat16 or wider, within the bound.
No kernel may reach another device: no remote copies, remote signals or barrier semaphores. Data moves between devices by JAX's collectives and lax.ppermute only.
A program may use at most 64 MiB of HBM per device.

```python
import jax
import jax.numpy as jnp
from jax import lax

HEADS = 24
HD = 128
DW = 3072
STEP = 10
TOKENS = 65536
HHD = 3072


def draw_second_moment(key, part):
    unit = jax.random.uniform(key, (DW, HEADS * HD), jnp.float32)
    return jnp.exp(jnp.log(0.1) + unit * jnp.log(10.0)) / TOKENS


def steps_of(rng, shape, split, least, largest):
    loudness = 1.0
    for axis_at, shards_of in split:
        steps = jax.random.uniform(jax.random.fold_in(jax.random.fold_in(rng, 6), axis_at), (shards_of,), jnp.float32, least / len(split), largest / len(split))
        loudness = loudness * jnp.repeat(jnp.exp(steps), shape[axis_at] // shards_of).reshape((-1,) + (1,) * (len(shape) - 1 - axis_at))
    return loudness


def gaussian(own_key, extent, scale, limit, shards=(), dtype=jnp.bfloat16):
    entries = jax.random.normal(own_key, extent, jnp.float32) * scale
    if len(shards) > 0:
        entries = steps_of(own_key, extent, shards, -0.22, 0.18) * entries
    return jnp.clip(entries, min=-limit, max=limit).astype(dtype)


def setup_inputs(seed: int = 0) -> dict:
    seeds = jax.random.split(jax.random.key(seed), 6)
    return {
        "cotangent": gaussian(seeds[0], (TOKENS, DW), 1.0, 6.0, ((0, 512),)),
        "context": gaussian(seeds[1], (TOKENS, HHD), 1.0, 6.0, ((0, 64), (1, 8))),
        "master": gaussian(seeds[2], (DW, HHD), HHD ** -0.5, 0.109375, ((0, 64), (1, 8)), jnp.float32),
        "first_moment": gaussian(seeds[3], (DW, HHD), TOKENS ** -0.5, 0.0234375, ((0, 64), (1, 8)), jnp.float32),
        "second_moment": draw_second_moment(jax.random.fold_in(seeds[5], 71), 0),
    }


def reference(cotangent, context, master, first_moment, second_moment):
    weights = master.astype(jnp.bfloat16)
    d_context = jnp.dot(cotangent, weights, preferred_element_type=jnp.float32).astype(jnp.bfloat16)
    total = lax.dot_general(cotangent, context, (((0,), (0,)), ((), ())), preferred_element_type=jnp.float32)
    grad = total / jnp.float32(TOKENS)
    new_first = 0.9 * first_moment + 0.1 * grad
    new_second = 0.95 * second_moment + 0.05 * grad * grad
    first_scale = 1.0 - 0.9 ** STEP
    second_scale = 1.0 - 0.95 ** STEP
    update = new_first / first_scale / (jnp.sqrt(new_second / second_scale) + 1e-08)
    new_master = master - 0.001 * update
    new_weights = new_master.astype(jnp.bfloat16)
    return (d_context, new_master, new_first, new_second, new_weights)
```

```python
import functools

import jax
import jax.numpy as jnp
from jax import lax
from jax.experimental import pallas as pl
from jax.experimental.pallas import tpu as pltpu
from jax.sharding import Mesh
from jax.sharding import PartitionSpec as P

STEP = 10
AXES = ("yl", "z", "c", "x", "yh")
SIZES = {"yl": 4, "z": 8, "c": 2, "x": 4, "yh": 2}
OWNED = 48
F32 = jnp.float32


def shift(value, axis, by):
    count = SIZES[axis]
    return lax.ppermute(value, axis, [(at, (at + by) % count) for at in range(count)])


def vmem():
    return pl.BlockSpec(memory_space=pltpu.VMEM)


def params():
    return pltpu.CompilerParams(vmem_limit_bytes=60 * 1024 * 1024)


def rows_of(refs, columns):
    return jnp.concatenate([ref[:, columns] for ref in refs], axis=0)


def grad_rows(refs, ctx_ref, slots, columns):
    ctx = jnp.concatenate([ctx_ref[slot] for slot in slots], axis=0)
    return lax.dot_general(
        rows_of(refs, columns), ctx, (((0,), (0,)), ((), ())), preferred_element_type=F32
    )


def first_grad(slots_ref, *refs):
    piece_refs, (ctx_ref, out_ref) = refs[:-2], refs[-2:]
    slots = [slots_ref[at] for at in range(4)]
    width = out_ref.shape[1]
    for line in range(out_ref.shape[0]):
        columns = slice(line * width, (line + 1) * width)
        out_ref[line] = grad_rows(piece_refs, ctx_ref, slots, columns)


def call_first_grad(pieces, ctx_blocks, slots):
    width, columns = pieces[0].shape[1] // 4, ctx_blocks.shape[2]
    smem = pl.BlockSpec(memory_space=pltpu.SMEM)
    return pl.pallas_call(
        first_grad,
        out_shape=jax.ShapeDtypeStruct((4, width, columns), F32),
        in_specs=[smem] + [vmem()] * (len(pieces) + 1),
        out_specs=vmem(),
        compiler_params=params(),
        name="first_grad",
    )(slots, *pieces, ctx_blocks)


def more_grad(slots_ref, *refs):
    piece_refs, (ctx_ref, sum_ref, out_ref) = refs[:-3], refs[-3:]
    slots = [slots_ref[at] for at in range(4, 7)]
    width = out_ref.shape[1]
    for line in range(out_ref.shape[0]):
        columns = slice(line * width, (line + 1) * width)
        out_ref[line] = sum_ref[line] + grad_rows(piece_refs, ctx_ref, slots, columns)


def call_more_grad(pieces, ctx_blocks, sums, slots):
    smem = pl.BlockSpec(memory_space=pltpu.SMEM)
    return pl.pallas_call(
        more_grad,
        out_shape=jax.ShapeDtypeStruct(sums.shape, F32),
        in_specs=[smem] + [vmem()] * (len(pieces) + 2),
        out_specs=vmem(),
        input_output_aliases={len(pieces) + 2: 0},
        compiler_params=params(),
        name="more_grad",
    )(slots, *pieces, ctx_blocks, sums)


def last_grad(slots_ref, core_ref, piece_ref, ctx_ref, sum_ref, keep_ref, give_ref):
    even_core = core_ref[0] == 0
    total = sum_ref[0] + grad_rows([piece_ref], ctx_ref, [slots_ref[7]], slice(None))
    for z in range(keep_ref.shape[0]):
        even = total[z * 2 * OWNED : z * 2 * OWNED + OWNED]
        odd = total[z * 2 * OWNED + OWNED : (z + 1) * 2 * OWNED]
        keep_ref[z] = jnp.where(even_core, even, odd)
        give_ref[z] = jnp.where(even_core, odd, even).astype(jnp.bfloat16)


def call_last_grad(piece, ctx_blocks, sums, slots, core):
    shape = (32, OWNED, ctx_blocks.shape[2])
    smem = pl.BlockSpec(memory_space=pltpu.SMEM)
    owned = pl.BlockSpec((8,) + shape[1:], lambda line: (line, 0, 0))
    return pl.pallas_call(
        last_grad,
        grid=(4,),
        out_shape=(jax.ShapeDtypeStruct(shape, F32), jax.ShapeDtypeStruct(shape, jnp.bfloat16)),
        in_specs=[
            smem,
            smem,
            pl.BlockSpec((128, sums.shape[1]), lambda line: (0, line)),
            pl.BlockSpec(ctx_blocks.shape, lambda line: (0, 0, 0)),
            pl.BlockSpec((1,) + sums.shape[1:], lambda line: (line, 0, 0)),
        ],
        out_specs=(owned, owned),
        compiler_params=params(),
        name="last_grad",
    )(slots, core, piece, ctx_blocks, sums)


def add_pair(keep_ref, given_ref, sum_ref):
    sum_ref[...] = (keep_ref[...] + given_ref[...].astype(F32)).astype(jnp.bfloat16)


def call_add_pair(keep, given):
    owned = pl.BlockSpec((8,) + given.shape[1:], lambda line: (line, 0, 0))
    return pl.pallas_call(
        add_pair,
        grid=(4,),
        out_shape=jax.ShapeDtypeStruct(given.shape, given.dtype),
        in_specs=[owned, owned],
        out_specs=owned,
        compiler_params=params(),
        name="add_pair",
    )(keep, given)


def token_rows(counts, slots_ref, *refs):
    w_ref, out_ref = refs[-2:]
    at = block = 0
    for count in counts:
        rows = jnp.dot(rows_of(refs[at : at + count], slice(None)), w_ref[...], preferred_element_type=F32)
        at += count
        for part in range(rows.shape[0] // 128):
            out_ref[slots_ref[block]] = rows[part * 128 : (part + 1) * 128].astype(jnp.bfloat16)
            block += 1


def call_token_rows(groups, weights, slots):
    columns = weights.shape[1]
    smem = pl.BlockSpec(memory_space=pltpu.SMEM)
    flat = [piece for group in groups for piece in group]
    return pl.pallas_call(
        functools.partial(token_rows, tuple(len(group) for group in groups)),
        out_shape=jax.ShapeDtypeStruct((8, 128, columns), jnp.bfloat16),
        in_specs=[smem] + [vmem()] * (len(flat) + 1),
        out_specs=vmem(),
        compiler_params=params(),
        name="token_rows",
    )(slots, *flat, weights)


def round_copies(value_ref, copies_ref):
    rounded = value_ref[...].astype(jnp.bfloat16)
    for at in range(copies_ref.shape[0]):
        copies_ref[at] = rounded


def call_round_copies(value):
    return pl.pallas_call(
        round_copies,
        out_shape=jax.ShapeDtypeStruct((4,) + value.shape, jnp.bfloat16),
        in_specs=[vmem()],
        out_specs=vmem(),
        compiler_params=params(),
        name="round_copies",
    )(value)


def adam(token_count, line_ref, w_ref, m_ref, v_ref, new_w_ref, new_m_ref, new_v_ref, copies_ref):
    total = line_ref[0].astype(F32)
    for at in range(1, line_ref.shape[0]):
        total += line_ref[at].astype(F32)
    grad = total / token_count
    new_first = 0.9 * m_ref[...] + 0.1 * grad
    new_second = 0.95 * v_ref[...] + 0.05 * grad * grad
    first_scale = 1.0 - 0.9**STEP
    second_scale = 1.0 - 0.95**STEP
    update = new_first / first_scale / (jnp.sqrt(new_second / second_scale) + 1e-08)
    new_master = w_ref[...] - 0.001 * update
    new_w_ref[...] = new_master
    new_m_ref[...] = new_first
    new_v_ref[...] = new_second
    rounded = new_master.astype(jnp.bfloat16)
    for at in range(copies_ref.shape[0]):
        copies_ref[at] = rounded


def call_adam(token_count, line, master, first_moment, second_moment):
    state = jax.ShapeDtypeStruct(master.shape, F32)
    return pl.pallas_call(
        functools.partial(adam, float(token_count)),
        out_shape=(state, state, state, jax.ShapeDtypeStruct((32,) + master.shape, jnp.bfloat16)),
        in_specs=[vmem()] * 4,
        out_specs=(vmem(),) * 4,
        compiler_params=params(),
        name="adam",
    )(line, master, first_moment, second_moment)


def interleave(core_ref, mine_ref, other_ref, out_ref):
    even_core = core_ref[0] == 0
    for at in range(mine_ref.shape[0]):
        mine, other = mine_ref[at], other_ref[at]
        out_ref[at, 0] = jnp.where(even_core, mine, other)
        out_ref[at, 1] = jnp.where(even_core, other, mine)


def both_cores(mine, core):
    other = shift(mine, "c", 1)
    columns = mine.shape[-1]
    owned = pl.BlockSpec((8, OWNED, columns), lambda line: (line, 0, 0))
    out = pl.pallas_call(
        interleave,
        out_shape=jax.ShapeDtypeStruct((32, 2, OWNED, columns), mine.dtype),
        grid=(4,),
        in_specs=[pl.BlockSpec(memory_space=pltpu.SMEM), owned, owned],
        out_specs=pl.BlockSpec((8, 2, OWNED, columns), lambda line: (line, 0, 0, 0)),
        compiler_params=params(),
        name="interleave",
    )(core, mine, other)
    return out.reshape(-1, columns)


def exchange(value, axes):
    return lax.all_to_all(value, axes, split_axis=0, concat_axis=0, tiled=True)


def step(cotangent, context, master, first_moment, second_moment):
    core = lax.axis_index("c").astype(jnp.int32).reshape(1)
    x = lax.axis_index("x").astype(jnp.int32)
    yh = lax.axis_index("yh").astype(jnp.int32)
    token_count = context.shape[0] * 64
    columns = context.shape[1]
    ctx_blocks = context.reshape(8, 128, columns)
    offsets = jnp.array([0, 3, 1, 2, 0, 3, 1, 2], jnp.int32)
    flips = jnp.array([0, 0, 0, 0, 1, 1, 1, 1], jnp.int32)
    slots = ((x + offsets) & 3) * 2 + (yh ^ flips)

    partner = shift(cotangent, "yh", 1)
    low, high = shift(cotangent, "x", 1), shift(cotangent, "x", -1)
    far = shift(cotangent, "x", 2)
    low_y, high_y = shift(partner, "x", 1), shift(partner, "x", -1)
    far_y = shift(partner, "x", 2)

    line = exchange(call_round_copies(master), ("yl",))
    planes = exchange(jnp.broadcast_to(line[None], (8,) + line.shape), ("z",))
    copies = planes.transpose(1, 0, 2, 3).reshape((32,) + master.shape)
    weights = both_cores(copies, core)

    sums = call_first_grad([cotangent, low, high, far], ctx_blocks, slots)
    sums = call_more_grad([partner, low_y, high_y], ctx_blocks, sums, slots)
    keep, give = call_last_grad(far_y, ctx_blocks, sums, slots, core)
    pair_sum = call_add_pair(keep, shift(give, "c", 1))
    received = exchange(pair_sum, ("yl", "z"))
    new_master, new_first, new_second, copies = call_adam(
        token_count, received, master, first_moment, second_moment
    )
    new_weights = both_cores(exchange(copies, ("yl", "z")), core)
    groups = [[cotangent, low], [high, far], [partner, low_y], [high_y, far_y]]
    d_context = call_token_rows(groups, weights, slots).reshape(-1, columns)
    return (d_context, new_master, new_first, new_second, new_weights)


def solution(mesh):
    fine = Mesh(mesh.devices.reshape(tuple(SIZES.values())), AXES)
    owner, part = ("yl", "z", "c"), ("x", "yh")
    in_specs = (P(owner + part, None),) + (P(owner, part),) * 4
    out_specs = (P(owner, part),) * 4 + (P(None, part),)
    return jax.shard_map(step, mesh=fine, in_specs=in_specs, out_specs=out_specs, check_vma=False)
```

```python
import functools

import jax
import jax.numpy as jnp
from jax import lax
from jax.experimental import pallas as pl
from jax.experimental.pallas import tpu as pltpu
from jax.sharding import Mesh
from jax.sharding import PartitionSpec as P

STEP = 10
AXES = ("yl", "z", "c", "x", "yh")
SIZES = {"yl": 4, "z": 8, "c": 2, "x": 4, "yh": 2}
OWNED = 48
F32 = jnp.float32


def shift(value, axis, by):
    count = SIZES[axis]
    return lax.ppermute(value, axis, [(at, (at + by) % count) for at in range(count)])


def vmem():
    return pl.BlockSpec(memory_space=pltpu.VMEM)


def on_chip(*values):
    return [pltpu.with_memory_space_constraint(value, pltpu.VMEM) for value in values]


def params():
    return pltpu.CompilerParams(vmem_limit_bytes=20 * 1024 * 1024)


def rows_of(refs, columns):
    return jnp.concatenate([ref[:, columns] for ref in refs], axis=0)


def grad_rows(refs, ctx_ref, slots, columns):
    ctx = jnp.concatenate([ctx_ref[slot] for slot in slots], axis=0)
    return lax.dot_general(
        rows_of(refs, columns), ctx, (((0,), (0,)), ((), ())), preferred_element_type=F32
    )


def first_grad(slots_ref, *refs):
    piece_refs, (ctx_ref, out_ref) = refs[:-2], refs[-2:]
    slots = [slots_ref[at] for at in range(4)]
    width = out_ref.shape[1]
    for line in range(out_ref.shape[0]):
        columns = slice(line * width, (line + 1) * width)
        out_ref[line] = grad_rows(piece_refs, ctx_ref, slots, columns)


def call_first_grad(pieces, ctx_blocks, slots):
    width, columns = pieces[0].shape[1] // 4, ctx_blocks.shape[2]
    smem = pl.BlockSpec(memory_space=pltpu.SMEM)
    return pl.pallas_call(
        first_grad,
        out_shape=pltpu.VMEM((4, width, columns), F32),
        in_specs=[smem] + [vmem()] * (len(pieces) + 1),
        out_specs=vmem(),
        compiler_params=params(),
        name="first_grad",
    )(slots, *on_chip(*pieces, ctx_blocks))


def more_grad(slots_ref, *refs):
    piece_refs, (ctx_ref, sum_ref, out_ref) = refs[:-3], refs[-3:]
    slots = [slots_ref[at] for at in range(4, 7)]
    width = out_ref.shape[1]
    for line in range(out_ref.shape[0]):
        columns = slice(line * width, (line + 1) * width)
        out_ref[line] = sum_ref[line] + grad_rows(piece_refs, ctx_ref, slots, columns)


def call_more_grad(pieces, ctx_blocks, sums, slots):
    smem = pl.BlockSpec(memory_space=pltpu.SMEM)
    return pl.pallas_call(
        more_grad,
        out_shape=pltpu.VMEM(sums.shape, F32),
        in_specs=[smem] + [vmem()] * (len(pieces) + 2),
        out_specs=vmem(),
        input_output_aliases={len(pieces) + 2: 0},
        compiler_params=params(),
        name="more_grad",
    )(slots, *on_chip(*pieces, ctx_blocks, sums))


def last_grad(slots_ref, core_ref, piece_ref, ctx_ref, sum_ref, keep_ref, give_ref):
    even_core = core_ref[0] == 0
    width = sum_ref.shape[1]
    for line in range(sum_ref.shape[0]):
        columns = slice(line * width, (line + 1) * width)
        total = sum_ref[line] + grad_rows([piece_ref], ctx_ref, [slots_ref[7]], columns)
        for z in range(8):
            even = total[z * 2 * OWNED : z * 2 * OWNED + OWNED]
            odd = total[z * 2 * OWNED + OWNED : (z + 1) * 2 * OWNED]
            keep_ref[line * 8 + z] = jnp.where(even_core, even, odd)
            give_ref[line * 8 + z] = jnp.where(even_core, odd, even).astype(jnp.bfloat16)


def call_last_grad(piece, ctx_blocks, sums, slots, core):
    shape = (32, OWNED, ctx_blocks.shape[2])
    smem = pl.BlockSpec(memory_space=pltpu.SMEM)
    return pl.pallas_call(
        last_grad,
        out_shape=(pltpu.VMEM(shape, F32), pltpu.VMEM(shape, jnp.bfloat16)),
        in_specs=[smem, smem] + [vmem()] * 3,
        out_specs=(vmem(), vmem()),
        compiler_params=params(),
        name="last_grad",
    )(slots, core, *on_chip(piece, ctx_blocks, sums))


def add_pair(keep_ref, given_ref, sum_ref):
    sum_ref[...] = (keep_ref[...] + given_ref[...].astype(F32)).astype(jnp.bfloat16)


def call_add_pair(keep, given):
    return pl.pallas_call(
        add_pair,
        out_shape=pltpu.VMEM(given.shape, given.dtype),
        in_specs=[vmem()] * 2,
        out_specs=vmem(),
        compiler_params=params(),
        name="add_pair",
    )(*on_chip(keep, given))


def token_rows(counts, slots_ref, *refs):
    w_ref, out_ref = refs[-2:]
    at = block = 0
    for count in counts:
        rows = jnp.dot(rows_of(refs[at : at + count], slice(None)), w_ref[...], preferred_element_type=F32)
        at += count
        for part in range(rows.shape[0] // 128):
            out_ref[slots_ref[block]] = rows[part * 128 : (part + 1) * 128].astype(jnp.bfloat16)
            block += 1


def call_token_rows(groups, weights, slots):
    columns = weights.shape[1]
    smem = pl.BlockSpec(memory_space=pltpu.SMEM)
    flat = [piece for group in groups for piece in group]
    return pl.pallas_call(
        functools.partial(token_rows, tuple(len(group) for group in groups)),
        out_shape=jax.ShapeDtypeStruct((8, 128, columns), jnp.bfloat16),
        in_specs=[smem] + [vmem()] * (len(flat) + 1),
        out_specs=vmem(),
        compiler_params=params(),
        name="token_rows",
    )(slots, *flat, weights)


def round_copies(value_ref, copies_ref):
    rounded = value_ref[...].astype(jnp.bfloat16)
    for at in range(copies_ref.shape[0]):
        copies_ref[at] = rounded


def call_round_copies(value):
    return pl.pallas_call(
        round_copies,
        out_shape=pltpu.VMEM((32,) + value.shape, jnp.bfloat16),
        in_specs=[vmem()],
        out_specs=vmem(),
        compiler_params=params(),
        name="round_copies",
    )(value)


def adam(token_count, line_ref, w_ref, m_ref, v_ref, new_w_ref, new_m_ref, new_v_ref, copies_ref):
    total = line_ref[0].astype(F32)
    for at in range(1, line_ref.shape[0]):
        total += line_ref[at].astype(F32)
    grad = total / token_count
    new_first = 0.9 * m_ref[...] + 0.1 * grad
    new_second = 0.95 * v_ref[...] + 0.05 * grad * grad
    first_scale = 1.0 - 0.9**STEP
    second_scale = 1.0 - 0.95**STEP
    update = new_first / first_scale / (jnp.sqrt(new_second / second_scale) + 1e-08)
    new_master = w_ref[...] - 0.001 * update
    new_w_ref[...] = new_master
    new_m_ref[...] = new_first
    new_v_ref[...] = new_second
    rounded = new_master.astype(jnp.bfloat16)
    for at in range(copies_ref.shape[0]):
        copies_ref[at] = rounded


def call_adam(token_count, line, master, first_moment, second_moment):
    state = jax.ShapeDtypeStruct(master.shape, F32)
    return pl.pallas_call(
        functools.partial(adam, float(token_count)),
        out_shape=(state, state, state, pltpu.VMEM((32,) + master.shape, jnp.bfloat16)),
        in_specs=[vmem()] * 4,
        out_specs=(vmem(),) * 4,
        compiler_params=params(),
        name="adam",
    )(*on_chip(line, master, first_moment, second_moment))


def interleave(core_ref, mine_ref, other_ref, out_ref):
    even_core = core_ref[0] == 0
    begin = pl.program_id(0) * out_ref.shape[0]
    for at in range(out_ref.shape[0]):
        mine, other = mine_ref[begin + at], other_ref[begin + at]
        out_ref[at, 0] = jnp.where(even_core, mine, other)
        out_ref[at, 1] = jnp.where(even_core, other, mine)


def both_cores(mine, core):
    other = shift(mine, "c", 1)
    columns = mine.shape[-1]
    out = pl.pallas_call(
        interleave,
        grid=(4,),
        out_shape=jax.ShapeDtypeStruct((32, 2, OWNED, columns), mine.dtype),
        in_specs=[pl.BlockSpec(memory_space=pltpu.SMEM), vmem(), vmem()],
        out_specs=pl.BlockSpec((8, 2, OWNED, columns), lambda line: (line, 0, 0, 0)),
        compiler_params=params(),
        name="interleave",
    )(core, *on_chip(mine, other))
    return out.reshape(-1, columns)


def exchange(value, axes):
    return lax.all_to_all(value, axes, split_axis=0, concat_axis=0, tiled=True)


def step(cotangent, context, master, first_moment, second_moment):
    core = lax.axis_index("c").astype(jnp.int32).reshape(1)
    x = lax.axis_index("x").astype(jnp.int32)
    yh = lax.axis_index("yh").astype(jnp.int32)
    token_count = context.shape[0] * 64
    columns = context.shape[1]
    ctx_blocks = context.reshape(8, 128, columns)
    offsets = jnp.array([0, 3, 1, 2, 0, 3, 1, 2], jnp.int32)
    flips = jnp.array([0, 0, 0, 0, 1, 1, 1, 1], jnp.int32)
    slots = ((x + offsets) & 3) * 2 + (yh ^ flips)

    partner = shift(cotangent, "yh", 1)
    low, high = shift(cotangent, "x", 1), shift(cotangent, "x", -1)
    far = shift(cotangent, "x", 2)
    low_y, high_y = shift(partner, "x", 1), shift(partner, "x", -1)
    far_y = shift(partner, "x", 2)

    copies = exchange(call_round_copies(master), ("yl", "z"))
    weights = both_cores(copies, core)

    sums = call_first_grad([cotangent, low, high, far], ctx_blocks, slots)
    sums = call_more_grad([partner, low_y, high_y], ctx_blocks, sums, slots)
    keep, give = call_last_grad(far_y, ctx_blocks, sums, slots, core)
    pair_sum = call_add_pair(keep, shift(give, "c", 1))
    received = exchange(pair_sum, ("yl", "z"))
    new_master, new_first, new_second, copies = call_adam(
        token_count, received, master, first_moment, second_moment
    )
    new_weights = both_cores(exchange(copies, ("yl", "z")), core)
    groups = [[cotangent, low], [high, far], [partner, low_y], [high_y, far_y]]
    d_context = call_token_rows(groups, weights, slots).reshape(-1, columns)
    return (d_context, new_master, new_first, new_second, new_weights)


def solution(mesh):
    fine = Mesh(mesh.devices.reshape(tuple(SIZES.values())), AXES)
    owner, part = ("yl", "z", "c"), ("x", "yh")
    in_specs = (P(owner + part, None),) + (P(owner, part),) * 4
    out_specs = (P(owner, part),) * 4 + (P(None, part),)
    return jax.shard_map(step, mesh=fine, in_specs=in_specs, out_specs=out_specs, check_vma=False)
```

```python
import functools

import jax
import jax.numpy as jnp
from jax import lax
from jax.experimental import pallas as pl
from jax.experimental.pallas import tpu as pltpu
from jax.sharding import Mesh
from jax.sharding import PartitionSpec as P

STEP = 10
AXES = ("yl", "z", "c", "x", "yh")
SIZES = {"yl": 4, "z": 8, "c": 2, "x": 4, "yh": 2}
OWNED = 48
F32 = jnp.float32


def shift(value, axis, by):
    count = SIZES[axis]
    return lax.ppermute(value, axis, [(at, (at + by) % count) for at in range(count)])


def vmem():
    return pl.BlockSpec(memory_space=pltpu.VMEM)


def on_chip(*values):
    return [pltpu.with_memory_space_constraint(value, pltpu.VMEM) for value in values]


def params():
    return pltpu.CompilerParams(vmem_limit_bytes=20 * 1024 * 1024)


def rows_of(refs, columns):
    return jnp.concatenate([ref[:, columns] for ref in refs], axis=0)


def grad_rows(refs, ctx_ref, slots, columns):
    ctx = jnp.concatenate([ctx_ref[slot] for slot in slots], axis=0)
    return lax.dot_general(
        rows_of(refs, columns), ctx, (((0,), (0,)), ((), ())), preferred_element_type=F32
    )


def first_grad(slots_ref, *refs):
    piece_refs, (ctx_ref, out_ref) = refs[:-2], refs[-2:]
    slots = [slots_ref[at] for at in range(4)]
    width = out_ref.shape[1]
    for line in range(out_ref.shape[0]):
        columns = slice(line * width, (line + 1) * width)
        out_ref[line] = grad_rows(piece_refs, ctx_ref, slots, columns)


def call_first_grad(pieces, ctx_blocks, slots):
    width, columns = pieces[0].shape[1] // 4, ctx_blocks.shape[2]
    smem = pl.BlockSpec(memory_space=pltpu.SMEM)
    return pl.pallas_call(
        first_grad,
        out_shape=pltpu.VMEM((4, width, columns), F32),
        in_specs=[smem] + [vmem()] * (len(pieces) + 1),
        out_specs=vmem(),
        compiler_params=params(),
        name="first_grad",
    )(slots, *on_chip(*pieces, ctx_blocks))


def more_grad(slots_ref, *refs):
    piece_refs, (ctx_ref, sum_ref, out_ref) = refs[:-3], refs[-3:]
    slots = [slots_ref[at] for at in range(4, 7)]
    width = out_ref.shape[1]
    for line in range(out_ref.shape[0]):
        columns = slice(line * width, (line + 1) * width)
        out_ref[line] = sum_ref[line] + grad_rows(piece_refs, ctx_ref, slots, columns)


def call_more_grad(pieces, ctx_blocks, sums, slots):
    smem = pl.BlockSpec(memory_space=pltpu.SMEM)
    return pl.pallas_call(
        more_grad,
        out_shape=pltpu.VMEM(sums.shape, F32),
        in_specs=[smem] + [vmem()] * (len(pieces) + 2),
        out_specs=vmem(),
        input_output_aliases={len(pieces) + 2: 0},
        compiler_params=params(),
        name="more_grad",
    )(slots, *on_chip(*pieces, ctx_blocks, sums))


def last_grad(slots_ref, core_ref, *refs):
    piece_refs, (ctx_ref, sum_ref, keep_ref, give_ref) = refs[:-4], refs[-4:]
    even_core = core_ref[0] == 0
    width = sum_ref.shape[1]
    for line in range(sum_ref.shape[0]):
        columns = slice(line * width, (line + 1) * width)
        total = sum_ref[line] + grad_rows(piece_refs, ctx_ref, [slots_ref[7]], columns)
        for z in range(8):
            even = total[z * 2 * OWNED : z * 2 * OWNED + OWNED]
            odd = total[z * 2 * OWNED + OWNED : (z + 1) * 2 * OWNED]
            keep_ref[line * 8 + z] = jnp.where(even_core, even, odd)
            give_ref[line * 8 + z] = jnp.where(even_core, odd, even).astype(jnp.bfloat16)


def call_last_grad(pieces, ctx_blocks, sums, slots, core):
    shape = (32, OWNED, ctx_blocks.shape[2])
    smem = pl.BlockSpec(memory_space=pltpu.SMEM)
    return pl.pallas_call(
        last_grad,
        out_shape=(pltpu.VMEM(shape, F32), pltpu.VMEM(shape, jnp.bfloat16)),
        in_specs=[smem, smem] + [vmem()] * (len(pieces) + 2),
        out_specs=(vmem(), vmem()),
        compiler_params=params(),
        name="last_grad",
    )(slots, core, *on_chip(*pieces, ctx_blocks, sums))


def add_pair(keep_ref, given_ref, sum_ref):
    sum_ref[...] = (keep_ref[...] + given_ref[...].astype(F32)).astype(jnp.bfloat16)


def call_add_pair(keep, given):
    return pl.pallas_call(
        add_pair,
        out_shape=pltpu.VMEM(given.shape, given.dtype),
        in_specs=[vmem()] * 2,
        out_specs=vmem(),
        compiler_params=params(),
        name="add_pair",
    )(*on_chip(keep, given))


def token_rows(counts, slots_ref, *refs):
    w_ref, out_ref = refs[-2:]
    at = block = 0
    for count in counts:
        rows = jnp.dot(rows_of(refs[at : at + count], slice(None)), w_ref[...], preferred_element_type=F32)
        at += count
        for part in range(rows.shape[0] // 128):
            out_ref[slots_ref[block]] = rows[part * 128 : (part + 1) * 128].astype(jnp.bfloat16)
            block += 1


def call_token_rows(groups, weights, slots):
    columns = weights.shape[1]
    smem = pl.BlockSpec(memory_space=pltpu.SMEM)
    flat = [piece for group in groups for piece in group]
    return pl.pallas_call(
        functools.partial(token_rows, tuple(len(group) for group in groups)),
        out_shape=jax.ShapeDtypeStruct((8, 128, columns), jnp.bfloat16),
        in_specs=[smem] + [vmem()] * (len(flat) + 1),
        out_specs=vmem(),
        compiler_params=params(),
        name="token_rows",
    )(slots, *flat, weights)


def halves(rows_ref, first_ref, second_ref):
    half = first_ref.shape[0]
    first_ref[...] = rows_ref[:half]
    second_ref[...] = rows_ref[half:]


def call_halves(rows):
    half = pltpu.VMEM((rows.shape[0] // 2, rows.shape[1]), rows.dtype)
    return pl.pallas_call(
        halves,
        out_shape=(half, half),
        in_specs=[vmem()],
        out_specs=(vmem(), vmem()),
        compiler_params=params(),
        name="halves",
    )(*on_chip(rows))


def adam(token_count, line_ref, w_ref, m_ref, v_ref, new_w_ref, new_m_ref, new_v_ref, copies_ref):
    total = line_ref[0].astype(F32)
    for at in range(1, line_ref.shape[0]):
        total += line_ref[at].astype(F32)
    grad = total / token_count
    new_first = 0.9 * m_ref[...] + 0.1 * grad
    new_second = 0.95 * v_ref[...] + 0.05 * grad * grad
    first_scale = 1.0 - 0.9**STEP
    second_scale = 1.0 - 0.95**STEP
    update = new_first / first_scale / (jnp.sqrt(new_second / second_scale) + 1e-08)
    new_master = w_ref[...] - 0.001 * update
    new_w_ref[...] = new_master
    new_m_ref[...] = new_first
    new_v_ref[...] = new_second
    rounded = new_master.astype(jnp.bfloat16)
    for at in range(copies_ref.shape[0]):
        copies_ref[at] = rounded


def call_adam(token_count, line, master, first_moment, second_moment):
    state = jax.ShapeDtypeStruct(master.shape, F32)
    return pl.pallas_call(
        functools.partial(adam, float(token_count)),
        out_shape=(state, state, state, pltpu.VMEM((32,) + master.shape, jnp.bfloat16)),
        in_specs=[vmem()] * 4,
        out_specs=(vmem(),) * 4,
        compiler_params=params(),
        name="adam",
    )(*on_chip(line, master, first_moment, second_moment))


def interleave(core_ref, mine_ref, other_ref, out_ref):
    even_core = core_ref[0] == 0
    line = pl.program_id(0)
    for z in range(8):
        at = (z, line) if len(mine_ref.shape) == 4 else line * 8 + z
        mine, other = mine_ref[at], other_ref[at]
        out_ref[z, 0] = jnp.where(even_core, mine, other)
        out_ref[z, 1] = jnp.where(even_core, other, mine)


def both_cores(mine, core):
    other = shift(mine, "c", 1)
    columns = mine.shape[-1]
    out = pl.pallas_call(
        interleave,
        grid=(4,),
        out_shape=jax.ShapeDtypeStruct((32, 2, OWNED, columns), mine.dtype),
        in_specs=[pl.BlockSpec(memory_space=pltpu.SMEM), vmem(), vmem()],
        out_specs=pl.BlockSpec((8, 2, OWNED, columns), lambda line: (line, 0, 0, 0)),
        compiler_params=params(),
        name="interleave",
    )(core, *on_chip(mine, other))
    return out.reshape(-1, columns)


def exchange(value, axes):
    return lax.all_to_all(value, axes, split_axis=0, concat_axis=0, tiled=True)


def step(cotangent, context, master, first_moment, second_moment):
    core = lax.axis_index("c").astype(jnp.int32).reshape(1)
    x = lax.axis_index("x").astype(jnp.int32)
    yh = lax.axis_index("yh").astype(jnp.int32)
    token_count = context.shape[0] * 64
    columns = context.shape[1]
    ctx_blocks = context.reshape(8, 128, columns)
    offsets = jnp.array([0, 3, 1, 2, 0, 3, 1, 2], jnp.int32)
    flips = jnp.array([0, 0, 0, 0, 1, 1, 1, 1], jnp.int32)
    slots = ((x + offsets) & 3) * 2 + (yh ^ flips)

    partner = shift(cotangent, "yh", 1)
    low, high = shift(cotangent, "x", 1), shift(cotangent, "x", -1)
    far = shift(cotangent, "x", 2)
    part_a, part_b = call_halves(partner)
    low_a, high_a = shift(part_a, "x", 1), shift(part_a, "x", -1)
    low_b, high_b = shift(part_b, "x", 1), shift(part_b, "x", -1)
    far_a, far_b = shift(high_a, "x", -1), shift(low_b, "x", 1)

    rounded = jnp.broadcast_to(master.astype(jnp.bfloat16)[None], (4,) + master.shape)
    line = exchange(rounded, ("yl",))
    planes = exchange(jnp.broadcast_to(line[None], (8,) + line.shape), ("z",))
    weights = both_cores(planes, core)

    sums = call_first_grad([cotangent, low, high, far], ctx_blocks, slots)
    sums = call_more_grad([partner, low_a, low_b, high_a, high_b], ctx_blocks, sums, slots)
    keep, give = call_last_grad([far_a, far_b], ctx_blocks, sums, slots, core)
    pair_sum = call_add_pair(keep, shift(give, "c", 1))
    received = exchange(pair_sum, ("yl", "z"))
    new_master, new_first, new_second, copies = call_adam(
        token_count, received, master, first_moment, second_moment
    )
    new_weights = both_cores(exchange(copies, ("yl", "z")), core)
    groups = [[cotangent, low], [high, far], [partner, low_a, low_b], [high_a, high_b, far_a, far_b]]
    d_context = call_token_rows(groups, weights, slots).reshape(-1, columns)
    return (d_context, new_master, new_first, new_second, new_weights)


def solution(mesh):
    fine = Mesh(mesh.devices.reshape(tuple(SIZES.values())), AXES)
    owner, part = ("yl", "z", "c"), ("x", "yh")
    in_specs = (P(owner + part, None),) + (P(owner, part),) * 4
    out_specs = (P(owner, part),) * 4 + (P(None, part),)
    return jax.shard_map(step, mesh=fine, in_specs=in_specs, out_specs=out_specs, check_vma=False)
```

```python
import functools

import jax
import jax.numpy as jnp
from jax import lax
from jax.experimental import pallas as pl
from jax.experimental.pallas import tpu as pltpu
from jax.sharding import Mesh
from jax.sharding import PartitionSpec as P

STEP = 10
AXES = ("yl", "z", "c", "x", "yh")
SIZES = {"yl": 4, "z": 8, "c": 2, "x": 4, "yh": 2}
OWNED = 48
F32 = jnp.float32


def shift(value, axis, by):
    count = SIZES[axis]
    return lax.ppermute(value, axis, [(at, (at + by) % count) for at in range(count)])


def vmem():
    return pl.BlockSpec(memory_space=pltpu.VMEM)


def on_chip(*values):
    return [pltpu.with_memory_space_constraint(value, pltpu.VMEM) for value in values]


def params():
    return pltpu.CompilerParams(vmem_limit_bytes=20 * 1024 * 1024)


def rows_of(refs, columns):
    return jnp.concatenate([ref[:, columns] for ref in refs], axis=0)


def grad_rows(refs, ctx_ref, slots, columns):
    ctx = jnp.concatenate([ctx_ref[slot] for slot in slots], axis=0)
    return lax.dot_general(
        rows_of(refs, columns), ctx, (((0,), (0,)), ((), ())), preferred_element_type=F32
    )


def first_grad(slots_ref, *refs):
    piece_refs, (ctx_ref, out_ref) = refs[:-2], refs[-2:]
    slots = [slots_ref[at] for at in range(4)]
    width = out_ref.shape[1]
    for line in range(out_ref.shape[0]):
        columns = slice(line * width, (line + 1) * width)
        out_ref[line] = grad_rows(piece_refs, ctx_ref, slots, columns)


def call_first_grad(pieces, ctx_blocks, slots):
    width, columns = pieces[0].shape[1] // 4, ctx_blocks.shape[2]
    smem = pl.BlockSpec(memory_space=pltpu.SMEM)
    return pl.pallas_call(
        first_grad,
        out_shape=pltpu.VMEM((4, width, columns), F32),
        in_specs=[smem] + [vmem()] * (len(pieces) + 1),
        out_specs=vmem(),
        compiler_params=params(),
        name="first_grad",
    )(slots, *on_chip(*pieces, ctx_blocks))


def more_grad(slots_ref, *refs):
    piece_refs, (ctx_ref, sum_ref, out_ref) = refs[:-3], refs[-3:]
    slots = [slots_ref[at] for at in range(4, 7)]
    width = out_ref.shape[1]
    for line in range(out_ref.shape[0]):
        columns = slice(line * width, (line + 1) * width)
        out_ref[line] = sum_ref[line] + grad_rows(piece_refs, ctx_ref, slots, columns)


def call_more_grad(pieces, ctx_blocks, sums, slots):
    smem = pl.BlockSpec(memory_space=pltpu.SMEM)
    return pl.pallas_call(
        more_grad,
        out_shape=pltpu.VMEM(sums.shape, F32),
        in_specs=[smem] + [vmem()] * (len(pieces) + 2),
        out_specs=vmem(),
        input_output_aliases={len(pieces) + 2: 0},
        compiler_params=params(),
        name="more_grad",
    )(slots, *on_chip(*pieces, ctx_blocks, sums))


def last_grad(slots_ref, core_ref, *refs):
    piece_refs, (ctx_ref, sum_ref, keep_ref, give_ref) = refs[:-4], refs[-4:]
    even_core = core_ref[0] == 0
    width = sum_ref.shape[1]
    for line in range(sum_ref.shape[0]):
        columns = slice(line * width, (line + 1) * width)
        total = sum_ref[line] + grad_rows(piece_refs, ctx_ref, [slots_ref[7]], columns)
        for z in range(8):
            even = total[z * 2 * OWNED : z * 2 * OWNED + OWNED]
            odd = total[z * 2 * OWNED + OWNED : (z + 1) * 2 * OWNED]
            keep_ref[line * 8 + z] = jnp.where(even_core, even, odd)
            give_ref[line * 8 + z] = jnp.where(even_core, odd, even).astype(jnp.bfloat16)


def call_last_grad(pieces, ctx_blocks, sums, slots, core):
    shape = (32, OWNED, ctx_blocks.shape[2])
    smem = pl.BlockSpec(memory_space=pltpu.SMEM)
    return pl.pallas_call(
        last_grad,
        out_shape=(pltpu.VMEM(shape, F32), pltpu.VMEM(shape, jnp.bfloat16)),
        in_specs=[smem, smem] + [vmem()] * (len(pieces) + 2),
        out_specs=(vmem(), vmem()),
        compiler_params=params(),
        name="last_grad",
    )(slots, core, *on_chip(*pieces, ctx_blocks, sums))


def add_pair(keep_ref, given_ref, sum_ref):
    sum_ref[...] = (keep_ref[...] + given_ref[...].astype(F32)).astype(jnp.bfloat16)


def call_add_pair(keep, given):
    return pl.pallas_call(
        add_pair,
        out_shape=pltpu.VMEM(given.shape, given.dtype),
        in_specs=[vmem()] * 2,
        out_specs=vmem(),
        compiler_params=params(),
        name="add_pair",
    )(*on_chip(keep, given))


def token_rows(counts, slots_ref, *refs):
    w_ref, out_ref = refs[-2:]
    at = block = 0
    for count in counts:
        rows = jnp.dot(rows_of(refs[at : at + count], slice(None)), w_ref[...], preferred_element_type=F32)
        at += count
        for part in range(rows.shape[0] // 128):
            out_ref[slots_ref[block]] = rows[part * 128 : (part + 1) * 128].astype(jnp.bfloat16)
            block += 1


def call_token_rows(groups, weights, slots):
    columns = weights.shape[1]
    smem = pl.BlockSpec(memory_space=pltpu.SMEM)
    flat = [piece for group in groups for piece in group]
    return pl.pallas_call(
        functools.partial(token_rows, tuple(len(group) for group in groups)),
        out_shape=jax.ShapeDtypeStruct((8, 128, columns), jnp.bfloat16),
        in_specs=[smem] + [vmem()] * (len(flat) + 1),
        out_specs=vmem(),
        compiler_params=params(),
        name="token_rows",
    )(slots, *flat, weights)


def adam(token_count, line_ref, w_ref, m_ref, v_ref, new_w_ref, new_m_ref, new_v_ref, copies_ref):
    total = line_ref[0].astype(F32)
    for at in range(1, line_ref.shape[0]):
        total += line_ref[at].astype(F32)
    grad = total / token_count
    new_first = 0.9 * m_ref[...] + 0.1 * grad
    new_second = 0.95 * v_ref[...] + 0.05 * grad * grad
    first_scale = 1.0 - 0.9**STEP
    second_scale = 1.0 - 0.95**STEP
    update = new_first / first_scale / (jnp.sqrt(new_second / second_scale) + 1e-08)
    new_master = w_ref[...] - 0.001 * update
    new_w_ref[...] = new_master
    new_m_ref[...] = new_first
    new_v_ref[...] = new_second
    rounded = new_master.astype(jnp.bfloat16)
    for at in range(copies_ref.shape[0]):
        copies_ref[at] = rounded


def call_adam(token_count, line, master, first_moment, second_moment):
    state = jax.ShapeDtypeStruct(master.shape, F32)
    return pl.pallas_call(
        functools.partial(adam, float(token_count)),
        out_shape=(state, state, state, pltpu.VMEM((32,) + master.shape, jnp.bfloat16)),
        in_specs=[vmem()] * 4,
        out_specs=(vmem(),) * 4,
        compiler_params=params(),
        name="adam",
    )(*on_chip(line, master, first_moment, second_moment))


def interleave(core_ref, mine_ref, other_ref, out_ref):
    even_core = core_ref[0] == 0
    line = pl.program_id(0)
    for z in range(8):
        at = (z, line) if len(mine_ref.shape) == 4 else line * 8 + z
        mine, other = mine_ref[at], other_ref[at]
        out_ref[z, 0] = jnp.where(even_core, mine, other)
        out_ref[z, 1] = jnp.where(even_core, other, mine)


def both_cores(mine, core):
    other = shift(mine, "c", 1)
    columns = mine.shape[-1]
    out = pl.pallas_call(
        interleave,
        grid=(4,),
        out_shape=jax.ShapeDtypeStruct((32, 2, OWNED, columns), mine.dtype),
        in_specs=[pl.BlockSpec(memory_space=pltpu.SMEM), vmem(), vmem()],
        out_specs=pl.BlockSpec((8, 2, OWNED, columns), lambda line: (line, 0, 0, 0)),
        compiler_params=params(),
        name="interleave",
    )(core, *on_chip(mine, other))
    return out.reshape(-1, columns)


def exchange(value, axes):
    return lax.all_to_all(value, axes, split_axis=0, concat_axis=0, tiled=True)


def step(cotangent, context, master, first_moment, second_moment):
    core = lax.axis_index("c").astype(jnp.int32).reshape(1)
    x = lax.axis_index("x").astype(jnp.int32)
    yh = lax.axis_index("yh").astype(jnp.int32)
    token_count = context.shape[0] * 64
    columns = context.shape[1]
    ctx_blocks = context.reshape(8, 128, columns)
    offsets = jnp.array([0, 3, 1, 2, 0, 3, 1, 2], jnp.int32)
    flips = jnp.array([0, 0, 0, 0, 1, 1, 1, 1], jnp.int32)
    slots = ((x + offsets) & 3) * 2 + (yh ^ flips)

    half = cotangent.shape[0] // 2
    part_a = shift(cotangent[:half], "yh", 1)
    part_b = shift(lax.optimization_barrier(cotangent)[half:], "yh", 1)
    low, high = shift(cotangent, "x", 1), shift(cotangent, "x", -1)
    far = shift(cotangent, "x", 2)
    low_a, high_a = shift(part_a, "x", 1), shift(part_a, "x", -1)
    low_b, high_b = shift(part_b, "x", 1), shift(part_b, "x", -1)
    far_a, far_b = shift(high_a, "x", -1), shift(low_b, "x", 1)

    rounded = jnp.broadcast_to(master.astype(jnp.bfloat16)[None], (4,) + master.shape)
    line = exchange(rounded, ("yl",))
    planes = exchange(jnp.broadcast_to(line[None], (8,) + line.shape), ("z",))
    weights = both_cores(planes, core)

    sums = call_first_grad([cotangent, low, high, far], ctx_blocks, slots)
    sums = call_more_grad([part_a, part_b, low_a, low_b, high_a, high_b], ctx_blocks, sums, slots)
    keep, give = call_last_grad([far_a, far_b], ctx_blocks, sums, slots, core)
    pair_sum = call_add_pair(keep, shift(give, "c", 1))
    received = exchange(pair_sum, ("yl", "z"))
    new_master, new_first, new_second, copies = call_adam(
        token_count, received, master, first_moment, second_moment
    )
    new_weights = both_cores(exchange(copies, ("yl", "z")), core)
    groups = [[cotangent, low], [high, far], [part_a, part_b, low_a, low_b], [high_a, high_b, far_a, far_b]]
    d_context = call_token_rows(groups, weights, slots).reshape(-1, columns)
    return (d_context, new_master, new_first, new_second, new_weights)


def solution(mesh):
    fine = Mesh(mesh.devices.reshape(tuple(SIZES.values())), AXES)
    owner, part = ("yl", "z", "c"), ("x", "yh")
    in_specs = (P(owner + part, None),) + (P(owner, part),) * 4
    out_specs = (P(owner, part),) * 4 + (P(None, part),)
    return jax.shard_map(step, mesh=fine, in_specs=in_specs, out_specs=out_specs, check_vma=False)
```

```python
import functools

import jax
import jax.numpy as jnp
from jax import lax
from jax.experimental import pallas as pl
from jax.experimental.pallas import tpu as pltpu
from jax.sharding import Mesh
from jax.sharding import PartitionSpec as P

STEP = 10
AXES = ("yl", "z", "c", "x", "yh")
SIZES = {"yl": 4, "z": 8, "c": 2, "x": 4, "yh": 2}
OWNED = 48
F32 = jnp.float32


def shift(value, axis, by):
    count = SIZES[axis]
    return lax.ppermute(value, axis, [(at, (at + by) % count) for at in range(count)])


def vmem():
    return pl.BlockSpec(memory_space=pltpu.VMEM)


def on_chip(*values):
    return [pltpu.with_memory_space_constraint(value, pltpu.VMEM) for value in values]


def params():
    return pltpu.CompilerParams(vmem_limit_bytes=20 * 1024 * 1024)


def rows_of(refs, columns):
    return jnp.concatenate([ref[:, columns] for ref in refs], axis=0)


def grad_rows(refs, ctx_ref, slots, columns):
    ctx = jnp.concatenate([ctx_ref[slot] for slot in slots], axis=0)
    return lax.dot_general(
        rows_of(refs, columns), ctx, (((0,), (0,)), ((), ())), preferred_element_type=F32
    )


def first_grad(slots_ref, *refs):
    piece_refs, (ctx_ref, out_ref) = refs[:-2], refs[-2:]
    slots = [slots_ref[at] for at in range(4)]
    width = out_ref.shape[1]
    for line in range(out_ref.shape[0]):
        columns = slice(line * width, (line + 1) * width)
        out_ref[line] = grad_rows(piece_refs, ctx_ref, slots, columns)


def call_first_grad(pieces, ctx_blocks, slots):
    width, columns = pieces[0].shape[1] // 4, ctx_blocks.shape[2]
    smem = pl.BlockSpec(memory_space=pltpu.SMEM)
    return pl.pallas_call(
        first_grad,
        out_shape=pltpu.VMEM((4, width, columns), F32),
        in_specs=[smem] + [vmem()] * (len(pieces) + 1),
        out_specs=vmem(),
        compiler_params=params(),
        name="first_grad",
    )(slots, *on_chip(*pieces, ctx_blocks))


def more_grad(slots_ref, *refs):
    piece_refs, (ctx_ref, sum_ref, out_ref) = refs[:-3], refs[-3:]
    slots = [slots_ref[at] for at in range(4, 7)]
    width = out_ref.shape[1]
    for line in range(out_ref.shape[0]):
        columns = slice(line * width, (line + 1) * width)
        out_ref[line] = sum_ref[line] + grad_rows(piece_refs, ctx_ref, slots, columns)


def call_more_grad(pieces, ctx_blocks, sums, slots):
    smem = pl.BlockSpec(memory_space=pltpu.SMEM)
    return pl.pallas_call(
        more_grad,
        out_shape=pltpu.VMEM(sums.shape, F32),
        in_specs=[smem] + [vmem()] * (len(pieces) + 2),
        out_specs=vmem(),
        input_output_aliases={len(pieces) + 2: 0},
        compiler_params=params(),
        name="more_grad",
    )(slots, *on_chip(*pieces, ctx_blocks, sums))


def last_grad(slots_ref, core_ref, *refs):
    piece_refs, (ctx_ref, sum_ref, keep_ref, give_ref) = refs[:-4], refs[-4:]
    even_core = core_ref[0] == 0
    width = sum_ref.shape[1]
    for line in range(sum_ref.shape[0]):
        columns = slice(line * width, (line + 1) * width)
        total = sum_ref[line] + grad_rows(piece_refs, ctx_ref, [slots_ref[7]], columns)
        for z in range(8):
            even = total[z * 2 * OWNED : z * 2 * OWNED + OWNED]
            odd = total[z * 2 * OWNED + OWNED : (z + 1) * 2 * OWNED]
            keep_ref[line * 8 + z] = jnp.where(even_core, even, odd)
            give_ref[line * 8 + z] = jnp.where(even_core, odd, even).astype(jnp.bfloat16)


def call_last_grad(pieces, ctx_blocks, sums, slots, core):
    shape = (32, OWNED, ctx_blocks.shape[2])
    smem = pl.BlockSpec(memory_space=pltpu.SMEM)
    return pl.pallas_call(
        last_grad,
        out_shape=(pltpu.VMEM(shape, F32), pltpu.VMEM(shape, jnp.bfloat16)),
        in_specs=[smem, smem] + [vmem()] * (len(pieces) + 2),
        out_specs=(vmem(), vmem()),
        compiler_params=params(),
        name="last_grad",
    )(slots, core, *on_chip(*pieces, ctx_blocks, sums))


def add_pair(keep_ref, given_ref, sum_ref):
    sum_ref[...] = (keep_ref[...] + given_ref[...].astype(F32)).astype(jnp.bfloat16)


def call_add_pair(keep, given):
    return pl.pallas_call(
        add_pair,
        out_shape=pltpu.VMEM(given.shape, given.dtype),
        in_specs=[vmem()] * 2,
        out_specs=vmem(),
        compiler_params=params(),
        name="add_pair",
    )(*on_chip(keep, given))


def token_rows(counts, slots_ref, *refs):
    w_ref, out_ref = refs[-2:]
    at = block = 0
    for count in counts:
        rows = jnp.dot(rows_of(refs[at : at + count], slice(None)), w_ref[...], preferred_element_type=F32)
        at += count
        for part in range(rows.shape[0] // 128):
            out_ref[slots_ref[block]] = rows[part * 128 : (part + 1) * 128].astype(jnp.bfloat16)
            block += 1


def call_token_rows(groups, weights, slots):
    columns = weights.shape[1]
    smem = pl.BlockSpec(memory_space=pltpu.SMEM)
    flat = [piece for group in groups for piece in group]
    return pl.pallas_call(
        functools.partial(token_rows, tuple(len(group) for group in groups)),
        out_shape=jax.ShapeDtypeStruct((8, 128, columns), jnp.bfloat16),
        in_specs=[smem] + [vmem()] * (len(flat) + 1),
        out_specs=vmem(),
        compiler_params=params(),
        name="token_rows",
    )(slots, *flat, weights)


def copies_of(count, value_ref, copies_ref):
    for at in range(count):
        copies_ref[at] = value_ref[...].astype(copies_ref.dtype)


def call_copies_of(count, value):
    return pl.pallas_call(
        functools.partial(copies_of, count),
        out_shape=pltpu.VMEM((count,) + value.shape, jnp.bfloat16),
        in_specs=[vmem()],
        out_specs=vmem(),
        compiler_params=params(),
    )(*on_chip(value))


def halves(upper_ref, lower_ref, upper_half_ref, lower_half_ref):
    half = upper_half_ref.shape[0]
    upper_half_ref[...] = upper_ref[:half]
    lower_half_ref[...] = lower_ref[half:]


def call_halves(upper, lower):
    half = pltpu.VMEM((upper.shape[0] // 2, upper.shape[1]), upper.dtype)
    return pl.pallas_call(
        halves,
        out_shape=(half, half),
        in_specs=[vmem()] * 2,
        out_specs=(vmem(), vmem()),
        compiler_params=params(),
        name="halves",
    )(*on_chip(upper, lower))


def adam(token_count, line_ref, w_ref, m_ref, v_ref, new_w_ref, new_m_ref, new_v_ref, copies_ref):
    total = line_ref[0].astype(F32)
    for at in range(1, line_ref.shape[0]):
        total += line_ref[at].astype(F32)
    grad = total / token_count
    new_first = 0.9 * m_ref[...] + 0.1 * grad
    new_second = 0.95 * v_ref[...] + 0.05 * grad * grad
    first_scale = 1.0 - 0.9**STEP
    second_scale = 1.0 - 0.95**STEP
    update = new_first / first_scale / (jnp.sqrt(new_second / second_scale) + 1e-08)
    new_master = w_ref[...] - 0.001 * update
    new_w_ref[...] = new_master
    new_m_ref[...] = new_first
    new_v_ref[...] = new_second
    rounded = new_master.astype(jnp.bfloat16)
    for at in range(copies_ref.shape[0]):
        copies_ref[at] = rounded


def call_adam(token_count, line, master, first_moment, second_moment):
    state = jax.ShapeDtypeStruct(master.shape, F32)
    return pl.pallas_call(
        functools.partial(adam, float(token_count)),
        out_shape=(state, state, state, pltpu.VMEM((32,) + master.shape, jnp.bfloat16)),
        in_specs=[vmem()] * 4,
        out_specs=(vmem(),) * 4,
        compiler_params=params(),
        name="adam",
    )(*on_chip(line, master, first_moment, second_moment))


def interleave(core_ref, mine_ref, other_ref, out_ref):
    even_core = core_ref[0] == 0
    line = pl.program_id(0)
    for z in range(8):
        at = (z, line) if len(mine_ref.shape) == 4 else line * 8 + z
        mine, other = mine_ref[at], other_ref[at]
        out_ref[z, 0] = jnp.where(even_core, mine, other)
        out_ref[z, 1] = jnp.where(even_core, other, mine)


def both_cores(mine, core):
    other = shift(mine, "c", 1)
    columns = mine.shape[-1]
    out = pl.pallas_call(
        interleave,
        grid=(4,),
        out_shape=jax.ShapeDtypeStruct((32, 2, OWNED, columns), mine.dtype),
        in_specs=[pl.BlockSpec(memory_space=pltpu.SMEM), vmem(), vmem()],
        out_specs=pl.BlockSpec((8, 2, OWNED, columns), lambda line: (line, 0, 0, 0)),
        compiler_params=params(),
        name="interleave",
    )(core, *on_chip(mine, other))
    return out.reshape(-1, columns)


def exchange(value, axes):
    return lax.all_to_all(value, axes, split_axis=0, concat_axis=0, tiled=True)


def step(cotangent, context, master, first_moment, second_moment):
    core = lax.axis_index("c").astype(jnp.int32).reshape(1)
    x = lax.axis_index("x").astype(jnp.int32)
    yh = lax.axis_index("yh").astype(jnp.int32)
    token_count = context.shape[0] * 64
    columns = context.shape[1]
    ctx_blocks = context.reshape(8, 128, columns)
    offsets = jnp.array([0, 3, 1, 2, 0, 3, 1, 2], jnp.int32)
    flips = jnp.array([0, 0, 0, 0, 1, 1, 1, 1], jnp.int32)
    slots = ((x + offsets) & 3) * 2 + (yh ^ flips)

    partner = shift(cotangent, "yh", 1)
    low, high = shift(cotangent, "x", 1), shift(cotangent, "x", -1)
    far = shift(cotangent, "x", 2)
    low_y, high_y = shift(partner, "x", 1), shift(partner, "x", -1)
    upper, lower = call_halves(far, partner)
    far_a, far_b = shift(upper, "yh", 1), shift(lower, "x", 2)

    line = exchange(call_copies_of(4, master), ("yl",))
    planes = exchange(call_copies_of(8, line), ("z",))
    weights = both_cores(planes, core)

    sums = call_first_grad([cotangent, low, high, far], ctx_blocks, slots)
    sums = call_more_grad([partner, low_y, high_y], ctx_blocks, sums, slots)
    keep, give = call_last_grad([far_a, far_b], ctx_blocks, sums, slots, core)
    pair_sum = call_add_pair(keep, shift(give, "c", 1))
    received = exchange(pair_sum, ("yl", "z"))
    new_master, new_first, new_second, copies = call_adam(
        token_count, received, master, first_moment, second_moment
    )
    new_weights = both_cores(exchange(copies, ("yl", "z")), core)
    groups = [[cotangent, low], [high, far], [partner, low_y], [high_y, far_a, far_b]]
    d_context = call_token_rows(groups, weights, slots).reshape(-1, columns)
    return (d_context, new_master, new_first, new_second, new_weights)


def solution(mesh):
    fine = Mesh(mesh.devices.reshape(tuple(SIZES.values())), AXES)
    owner, part = ("yl", "z", "c"), ("x", "yh")
    in_specs = (P(owner + part, None),) + (P(owner, part),) * 4
    out_specs = (P(owner, part),) * 4 + (P(None, part),)
    return jax.shard_map(step, mesh=fine, in_specs=in_specs, out_specs=out_specs, check_vma=False)
```

```python
import functools

import jax
import jax.numpy as jnp
from jax import lax
from jax.experimental import pallas as pl
from jax.experimental.pallas import tpu as pltpu
from jax.sharding import Mesh
from jax.sharding import PartitionSpec as P

STEP = 10
AXES = ("yl", "z", "c", "x", "yh")
SIZES = {"yl": 4, "z": 8, "c": 2, "x": 4, "yh": 2}
OWNED = 48
OVER_Y = 48
F32 = jnp.float32


def shift(value, axis, by):
    count = SIZES[axis]
    return lax.ppermute(value, axis, [(at, (at + by) % count) for at in range(count)])


def vmem():
    return pl.BlockSpec(memory_space=pltpu.VMEM)


def on_chip(*values):
    return [pltpu.with_memory_space_constraint(value, pltpu.VMEM) for value in values]


def params():
    return pltpu.CompilerParams(vmem_limit_bytes=20 * 1024 * 1024)


def rows_of(refs, columns):
    return jnp.concatenate([ref[:, columns] for ref in refs], axis=0)


def grad_rows(refs, ctx_ref, slots, columns):
    ctx = jnp.concatenate([ctx_ref[slot] for slot in slots], axis=0)
    return lax.dot_general(
        rows_of(refs, columns), ctx, (((0,), (0,)), ((), ())), preferred_element_type=F32
    )


def first_grad(slots_ref, *refs):
    piece_refs, (ctx_ref, out_ref) = refs[:-2], refs[-2:]
    slots = [slots_ref[at] for at in range(7)]
    width = out_ref.shape[1]
    for line in range(out_ref.shape[0]):
        columns = slice(line * width, (line + 1) * width)
        out_ref[line] = grad_rows(piece_refs, ctx_ref, slots, columns)


def call_first_grad(pieces, ctx_blocks, slots):
    width, columns = pieces[0].shape[1] // 4, ctx_blocks.shape[2]
    smem = pl.BlockSpec(memory_space=pltpu.SMEM)
    return pl.pallas_call(
        first_grad,
        out_shape=pltpu.VMEM((4, width, columns), F32),
        in_specs=[smem] + [vmem()] * (len(pieces) + 1),
        out_specs=vmem(),
        compiler_params=params(),
        name="first_grad",
    )(slots, *on_chip(*pieces, ctx_blocks))


def last_grad(slots_ref, core_ref, *refs):
    piece_refs, (ctx_ref, sum_ref, keep_ref, give_ref) = refs[:-4], refs[-4:]
    even_core = core_ref[0] == 0
    width = sum_ref.shape[1]
    for line in range(sum_ref.shape[0]):
        columns = slice(line * width, (line + 1) * width)
        total = sum_ref[line] + grad_rows(piece_refs, ctx_ref, [slots_ref[7]], columns)
        for z in range(8):
            even = total[z * 2 * OWNED : z * 2 * OWNED + OWNED]
            odd = total[z * 2 * OWNED + OWNED : (z + 1) * 2 * OWNED]
            keep_ref[line * 8 + z] = jnp.where(even_core, even, odd)
            give_ref[line * 8 + z] = jnp.where(even_core, odd, even).astype(jnp.bfloat16)


def call_last_grad(pieces, ctx_blocks, sums, slots, core):
    shape = (32, OWNED, ctx_blocks.shape[2])
    smem = pl.BlockSpec(memory_space=pltpu.SMEM)
    return pl.pallas_call(
        last_grad,
        out_shape=(pltpu.VMEM(shape, F32), pltpu.VMEM(shape, jnp.bfloat16)),
        in_specs=[smem, smem] + [vmem()] * (len(pieces) + 2),
        out_specs=(vmem(), vmem()),
        compiler_params=params(),
        name="last_grad",
    )(slots, core, *on_chip(*pieces, ctx_blocks, sums))


def add_pair(keep_ref, given_ref, sum_ref):
    sum_ref[...] = (keep_ref[...] + given_ref[...].astype(F32)).astype(jnp.bfloat16)


def call_add_pair(keep, given):
    return pl.pallas_call(
        add_pair,
        out_shape=pltpu.HBM(given.shape, given.dtype),
        in_specs=[vmem()] * 2,
        out_specs=vmem(),
        compiler_params=params(),
        name="add_pair",
    )(*on_chip(keep, given))


def token_rows(counts, slots_ref, *refs):
    w_ref, out_ref = refs[-2:]
    at = block = 0
    for count in counts:
        rows = jnp.dot(rows_of(refs[at : at + count], slice(None)), w_ref[...], preferred_element_type=F32)
        at += count
        for part in range(rows.shape[0] // 128):
            out_ref[slots_ref[block]] = rows[part * 128 : (part + 1) * 128].astype(jnp.bfloat16)
            block += 1


def call_token_rows(groups, weights, slots):
    columns = weights.shape[1]
    smem = pl.BlockSpec(memory_space=pltpu.SMEM)
    flat = [piece for group in groups for piece in group]
    return pl.pallas_call(
        functools.partial(token_rows, tuple(len(group) for group in groups)),
        out_shape=jax.ShapeDtypeStruct((8, 128, columns), jnp.bfloat16),
        in_specs=[smem] + [vmem()] * (len(flat) + 1),
        out_specs=vmem(),
        compiler_params=params(),
        name="token_rows",
    )(slots, *flat, weights)


def copies_of(count, value_ref, copies_ref):
    for at in range(count):
        copies_ref[at] = value_ref[...].astype(copies_ref.dtype)


def call_copies_of(count, value):
    return pl.pallas_call(
        functools.partial(copies_of, count),
        out_shape=pltpu.HBM((count,) + value.shape, jnp.bfloat16),
        in_specs=[vmem()],
        out_specs=vmem(),
        compiler_params=params(),
    )(*on_chip(value))


def halves(upper_ref, lower_ref, upper_half_ref, lower_half_ref):
    upper_half_ref[...] = upper_ref[:OVER_Y]
    lower_half_ref[...] = lower_ref[OVER_Y:]


def call_halves(upper, lower):
    rows, columns = upper.shape
    return pl.pallas_call(
        halves,
        out_shape=(
            pltpu.VMEM((OVER_Y, columns), upper.dtype),
            pltpu.VMEM((rows - OVER_Y, columns), lower.dtype),
        ),
        in_specs=[vmem()] * 2,
        out_specs=(vmem(), vmem()),
        compiler_params=params(),
        name="halves",
    )(*on_chip(upper, lower))


def adam(token_count, line_ref, w_ref, m_ref, v_ref, new_w_ref, new_m_ref, new_v_ref, copies_ref):
    total = line_ref[0].astype(F32)
    for at in range(1, line_ref.shape[0]):
        total += line_ref[at].astype(F32)
    grad = total / token_count
    new_first = 0.9 * m_ref[...] + 0.1 * grad
    new_second = 0.95 * v_ref[...] + 0.05 * grad * grad
    first_scale = 1.0 - 0.9**STEP
    second_scale = 1.0 - 0.95**STEP
    update = new_first / first_scale / (jnp.sqrt(new_second / second_scale) + 1e-08)
    new_master = w_ref[...] - 0.001 * update
    new_w_ref[...] = new_master
    new_m_ref[...] = new_first
    new_v_ref[...] = new_second
    rounded = new_master.astype(jnp.bfloat16)
    for at in range(copies_ref.shape[0]):
        copies_ref[at] = rounded


def call_adam(token_count, line, master, first_moment, second_moment):
    state = jax.ShapeDtypeStruct(master.shape, F32)
    return pl.pallas_call(
        functools.partial(adam, float(token_count)),
        out_shape=(state, state, state, pltpu.HBM((32,) + master.shape, jnp.bfloat16)),
        in_specs=[vmem()] * 4,
        out_specs=(vmem(),) * 4,
        compiler_params=params(),
        name="adam",
    )(*on_chip(line, master, first_moment, second_moment))


def interleave(core_ref, mine_ref, other_ref, out_ref):
    even_core = core_ref[0] == 0
    line = pl.program_id(0)
    for z in range(8):
        at = (z, line) if len(mine_ref.shape) == 4 else line * 8 + z
        mine, other = mine_ref[at], other_ref[at]
        out_ref[z, 0] = jnp.where(even_core, mine, other)
        out_ref[z, 1] = jnp.where(even_core, other, mine)


def both_cores(mine, core):
    other = shift(mine, "c", 1)
    columns = mine.shape[-1]
    out = pl.pallas_call(
        interleave,
        grid=(4,),
        out_shape=jax.ShapeDtypeStruct((32, 2, OWNED, columns), mine.dtype),
        in_specs=[pl.BlockSpec(memory_space=pltpu.SMEM), vmem(), vmem()],
        out_specs=pl.BlockSpec((8, 2, OWNED, columns), lambda line: (line, 0, 0, 0)),
        compiler_params=params(),
        name="interleave",
    )(core, *on_chip(mine, other))
    return out.reshape(-1, columns)


def exchange(value, axes):
    return lax.all_to_all(value, axes, split_axis=0, concat_axis=0, tiled=True)


def step(cotangent, context, master, first_moment, second_moment):
    core = lax.axis_index("c").astype(jnp.int32).reshape(1)
    x = lax.axis_index("x").astype(jnp.int32)
    yh = lax.axis_index("yh").astype(jnp.int32)
    token_count = context.shape[0] * 64
    columns = context.shape[1]
    ctx_blocks = context.reshape(8, 128, columns)
    offsets = jnp.array([0, 3, 1, 2, 0, 3, 1, 2], jnp.int32)
    flips = jnp.array([0, 0, 0, 0, 1, 1, 1, 1], jnp.int32)
    slots = ((x + offsets) & 3) * 2 + (yh ^ flips)

    partner = shift(cotangent, "yh", 1)
    low, high = shift(cotangent, "x", 1), shift(cotangent, "x", -1)
    far = shift(cotangent, "x", 2)
    low_y, high_y = shift(partner, "x", 1), shift(partner, "x", -1)
    upper, lower = call_halves(far, partner)
    far_a, far_b = shift(upper, "yh", 1), shift(lower, "x", 2)

    line = exchange(call_copies_of(4, master), ("yl",))
    planes = exchange(call_copies_of(8, line), ("z",))
    weights = both_cores(planes, core)

    early = [cotangent, low, high, far, partner, low_y, high_y]
    sums = call_first_grad(early, ctx_blocks, slots)
    keep, give = call_last_grad([far_a, far_b], ctx_blocks, sums, slots, core)
    pair_sum = call_add_pair(keep, shift(give, "c", 1))
    received = exchange(pair_sum, ("yl", "z"))
    new_master, new_first, new_second, copies = call_adam(
        token_count, received, master, first_moment, second_moment
    )
    new_weights = both_cores(exchange(copies, ("yl", "z")), core)
    groups = [[cotangent, low], [high, far], [partner, low_y], [high_y, far_a, far_b]]
    d_context = call_token_rows(groups, weights, slots).reshape(-1, columns)
    return (d_context, new_master, new_first, new_second, new_weights)


def solution(mesh):
    fine = Mesh(mesh.devices.reshape(tuple(SIZES.values())), AXES)
    owner, part = ("yl", "z", "c"), ("x", "yh")
    in_specs = (P(owner + part, None),) + (P(owner, part),) * 4
    out_specs = (P(owner, part),) * 4 + (P(None, part),)
    return jax.shard_map(step, mesh=fine, in_specs=in_specs, out_specs=out_specs, check_vma=False)
```

```python
import functools

import jax
import jax.numpy as jnp
from jax import lax
from jax.experimental import pallas as pl
from jax.experimental.pallas import tpu as pltpu
from jax.sharding import Mesh
from jax.sharding import PartitionSpec as P

STEP = 10
AXES = ("yl", "z", "c", "x", "yh")
SIZES = {"yl": 4, "z": 8, "c": 2, "x": 4, "yh": 2}
OWNED = 48
OVER_Y = 48
F32 = jnp.float32


def shift(value, axis, by):
    count = SIZES[axis]
    return lax.ppermute(value, axis, [(at, (at + by) % count) for at in range(count)])


def vmem():
    return pl.BlockSpec(memory_space=pltpu.VMEM)


def on_chip(*values):
    return [pltpu.with_memory_space_constraint(value, pltpu.VMEM) for value in values]


def params():
    return pltpu.CompilerParams(vmem_limit_bytes=20 * 1024 * 1024)


def rows_of(refs, columns):
    return jnp.concatenate([ref[:, columns] for ref in refs], axis=0)


def grad_rows(refs, ctx_ref, slots, columns):
    ctx = jnp.concatenate([ctx_ref[slot] for slot in slots], axis=0)
    return lax.dot_general(
        rows_of(refs, columns), ctx, (((0,), (0,)), ((), ())), preferred_element_type=F32
    )


def first_grad(slots_ref, *refs):
    piece_refs, (ctx_ref, out_ref) = refs[:-2], refs[-2:]
    slots = [slots_ref[at] for at in range(5)]
    width = out_ref.shape[1]
    for line in range(out_ref.shape[0]):
        columns = slice(line * width, (line + 1) * width)
        out_ref[line] = grad_rows(piece_refs, ctx_ref, slots, columns)


def call_first_grad(pieces, ctx_blocks, slots):
    width, columns = pieces[0].shape[1] // 4, ctx_blocks.shape[2]
    smem = pl.BlockSpec(memory_space=pltpu.SMEM)
    return pl.pallas_call(
        first_grad,
        out_shape=pltpu.VMEM((4, width, columns), F32),
        in_specs=[smem] + [vmem()] * (len(pieces) + 1),
        out_specs=vmem(),
        compiler_params=params(),
        name="first_grad",
    )(slots, *on_chip(*pieces, ctx_blocks))


def last_grad(slots_ref, core_ref, *refs):
    piece_refs, (ctx_ref, sum_ref, keep_ref, give_ref) = refs[:-4], refs[-4:]
    even_core = core_ref[0] == 0
    slots = [slots_ref[at] for at in range(5, 8)]
    width = sum_ref.shape[1]
    for line in range(sum_ref.shape[0]):
        columns = slice(line * width, (line + 1) * width)
        total = sum_ref[line] + grad_rows(piece_refs, ctx_ref, slots, columns)
        for z in range(8):
            even = total[z * 2 * OWNED : z * 2 * OWNED + OWNED]
            odd = total[z * 2 * OWNED + OWNED : (z + 1) * 2 * OWNED]
            keep_ref[line * 8 + z] = jnp.where(even_core, even, odd)
            give_ref[line * 8 + z] = jnp.where(even_core, odd, even).astype(jnp.bfloat16)


def call_last_grad(pieces, ctx_blocks, sums, slots, core):
    shape = (32, OWNED, ctx_blocks.shape[2])
    smem = pl.BlockSpec(memory_space=pltpu.SMEM)
    return pl.pallas_call(
        last_grad,
        out_shape=(pltpu.VMEM(shape, F32), pltpu.VMEM(shape, jnp.bfloat16)),
        in_specs=[smem, smem] + [vmem()] * (len(pieces) + 2),
        out_specs=(vmem(), vmem()),
        compiler_params=params(),
        name="last_grad",
    )(slots, core, *on_chip(*pieces, ctx_blocks, sums))


def add_pair(keep_ref, given_ref, sum_ref):
    sum_ref[...] = (keep_ref[...] + given_ref[...].astype(F32)).astype(jnp.bfloat16)


def call_add_pair(keep, given):
    return pl.pallas_call(
        add_pair,
        out_shape=pltpu.HBM(given.shape, given.dtype),
        in_specs=[vmem()] * 2,
        out_specs=vmem(),
        compiler_params=params(),
        name="add_pair",
    )(*on_chip(keep, given))


def token_rows(counts, slots_ref, *refs):
    w_ref, out_ref = refs[-2:]
    at = block = 0
    for count in counts:
        rows = jnp.dot(rows_of(refs[at : at + count], slice(None)), w_ref[...], preferred_element_type=F32)
        at += count
        for part in range(rows.shape[0] // 128):
            out_ref[slots_ref[block]] = rows[part * 128 : (part + 1) * 128].astype(jnp.bfloat16)
            block += 1


def call_token_rows(groups, weights, slots):
    columns = weights.shape[1]
    smem = pl.BlockSpec(memory_space=pltpu.SMEM)
    flat = [piece for group in groups for piece in group]
    return pl.pallas_call(
        functools.partial(token_rows, tuple(len(group) for group in groups)),
        out_shape=jax.ShapeDtypeStruct((8, 128, columns), jnp.bfloat16),
        in_specs=[smem] + [vmem()] * (len(flat) + 1),
        out_specs=vmem(),
        compiler_params=params(),
        name="token_rows",
    )(slots, *flat, weights)


def copies_of(count, value_ref, copies_ref):
    for at in range(count):
        copies_ref[at] = value_ref[...].astype(copies_ref.dtype)


def call_copies_of(count, value):
    return pl.pallas_call(
        functools.partial(copies_of, count),
        out_shape=pltpu.HBM((count,) + value.shape, jnp.bfloat16),
        in_specs=[vmem()],
        out_specs=vmem(),
        compiler_params=params(),
    )(*on_chip(value))


def halves(upper_ref, lower_ref, upper_half_ref, lower_half_ref):
    upper_half_ref[...] = upper_ref[:OVER_Y]
    lower_half_ref[...] = lower_ref[OVER_Y:]


def call_halves(upper, lower):
    rows, columns = upper.shape
    return pl.pallas_call(
        halves,
        out_shape=(
            pltpu.VMEM((OVER_Y, columns), upper.dtype),
            pltpu.VMEM((rows - OVER_Y, columns), lower.dtype),
        ),
        in_specs=[vmem()] * 2,
        out_specs=(vmem(), vmem()),
        compiler_params=params(),
        name="halves",
    )(*on_chip(upper, lower))


def adam(token_count, line_ref, w_ref, m_ref, v_ref, new_w_ref, new_m_ref, new_v_ref, copies_ref):
    total = line_ref[0].astype(F32)
    for at in range(1, line_ref.shape[0]):
        total += line_ref[at].astype(F32)
    grad = total / token_count
    new_first = 0.9 * m_ref[...] + 0.1 * grad
    new_second = 0.95 * v_ref[...] + 0.05 * grad * grad
    first_scale = 1.0 - 0.9**STEP
    second_scale = 1.0 - 0.95**STEP
    update = new_first / first_scale / (jnp.sqrt(new_second / second_scale) + 1e-08)
    new_master = w_ref[...] - 0.001 * update
    new_w_ref[...] = new_master
    new_m_ref[...] = new_first
    new_v_ref[...] = new_second
    rounded = new_master.astype(jnp.bfloat16)
    for at in range(copies_ref.shape[0]):
        copies_ref[at] = rounded


def call_adam(token_count, line, master, first_moment, second_moment):
    state = jax.ShapeDtypeStruct(master.shape, F32)
    return pl.pallas_call(
        functools.partial(adam, float(token_count)),
        out_shape=(state, state, state, pltpu.HBM((32,) + master.shape, jnp.bfloat16)),
        in_specs=[vmem()] * 4,
        out_specs=(vmem(),) * 4,
        compiler_params=params(),
        name="adam",
    )(*on_chip(line, master, first_moment, second_moment))


def interleave(core_ref, mine_ref, other_ref, out_ref):
    even_core = core_ref[0] == 0
    line = pl.program_id(0)
    for z in range(8):
        at = (z, line) if len(mine_ref.shape) == 4 else line * 8 + z
        mine, other = mine_ref[at], other_ref[at]
        out_ref[z, 0] = jnp.where(even_core, mine, other)
        out_ref[z, 1] = jnp.where(even_core, other, mine)


def both_cores(mine, core):
    other = shift(mine, "c", 1)
    columns = mine.shape[-1]
    out = pl.pallas_call(
        interleave,
        grid=(4,),
        out_shape=jax.ShapeDtypeStruct((32, 2, OWNED, columns), mine.dtype),
        in_specs=[pl.BlockSpec(memory_space=pltpu.SMEM), vmem(), vmem()],
        out_specs=pl.BlockSpec((8, 2, OWNED, columns), lambda line: (line, 0, 0, 0)),
        compiler_params=params(),
        name="interleave",
    )(core, *on_chip(mine, other))
    return out.reshape(-1, columns)


def exchange(value, axes):
    return lax.all_to_all(value, axes, split_axis=0, concat_axis=0, tiled=True)


def step(cotangent, context, master, first_moment, second_moment):
    core = lax.axis_index("c").astype(jnp.int32).reshape(1)
    x = lax.axis_index("x").astype(jnp.int32)
    yh = lax.axis_index("yh").astype(jnp.int32)
    token_count = context.shape[0] * 64
    columns = context.shape[1]
    ctx_blocks = context.reshape(8, 128, columns)
    offsets = jnp.array([0, 3, 1, 2, 0, 3, 1, 2], jnp.int32)
    flips = jnp.array([0, 0, 0, 0, 1, 1, 1, 1], jnp.int32)
    slots = ((x + offsets) & 3) * 2 + (yh ^ flips)

    partner = shift(cotangent, "yh", 1)
    low, high = shift(cotangent, "x", 1), shift(cotangent, "x", -1)
    far = shift(cotangent, "x", 2)
    low_y, high_y = shift(partner, "x", 1), shift(partner, "x", -1)
    upper, lower = call_halves(far, partner)
    far_a, far_b = shift(upper, "yh", 1), shift(lower, "x", 2)

    line = exchange(call_copies_of(4, master), ("yl",))
    planes = exchange(call_copies_of(8, line), ("z",))
    weights = both_cores(planes, core)

    early = [cotangent, low, high, far, partner]
    sums = call_first_grad(early, ctx_blocks, slots)
    keep, give = call_last_grad([low_y, high_y, far_a, far_b], ctx_blocks, sums, slots, core)
    pair_sum = call_add_pair(keep, shift(give, "c", 1))
    received = exchange(pair_sum, ("yl", "z"))
    new_master, new_first, new_second, copies = call_adam(
        token_count, received, master, first_moment, second_moment
    )
    new_weights = both_cores(exchange(copies, ("yl", "z")), core)
    groups = [[cotangent, low], [high, far], [partner, low_y], [high_y, far_a, far_b]]
    d_context = call_token_rows(groups, weights, slots).reshape(-1, columns)
    return (d_context, new_master, new_first, new_second, new_weights)


def solution(mesh):
    fine = Mesh(mesh.devices.reshape(tuple(SIZES.values())), AXES)
    owner, part = ("yl", "z", "c"), ("x", "yh")
    in_specs = (P(owner + part, None),) + (P(owner, part),) * 4
    out_specs = (P(owner, part),) * 4 + (P(None, part),)
    return jax.shard_map(step, mesh=fine, in_specs=in_specs, out_specs=out_specs, check_vma=False)
```

```python
import functools

import jax
import jax.numpy as jnp
from jax import lax
from jax.experimental import pallas as pl
from jax.experimental.pallas import tpu as pltpu
from jax.sharding import Mesh
from jax.sharding import PartitionSpec as P

STEP = 10
AXES = ("yl", "z", "c", "x", "yh")
SIZES = {"yl": 4, "z": 8, "c": 2, "x": 4, "yh": 2}
OWNED = 48
OVER_Y = 48
F32 = jnp.float32


def shift(value, axis, by):
    count = SIZES[axis]
    return lax.ppermute(value, axis, [(at, (at + by) % count) for at in range(count)])


def vmem():
    return pl.BlockSpec(memory_space=pltpu.VMEM)


def on_chip(*values):
    return [pltpu.with_memory_space_constraint(value, pltpu.VMEM) for value in values]


def params():
    return pltpu.CompilerParams(vmem_limit_bytes=20 * 1024 * 1024)


def rows_of(refs, columns):
    return jnp.concatenate([ref[:, columns] for ref in refs], axis=0)


def grad_rows(refs, ctx_ref, slots, columns):
    ctx = jnp.concatenate([ctx_ref[slot] for slot in slots], axis=0)
    return lax.dot_general(
        rows_of(refs, columns), ctx, (((0,), (0,)), ((), ())), preferred_element_type=F32
    )


def first_grad(slots_ref, *refs):
    piece_refs, (ctx_ref, out_ref) = refs[:-2], refs[-2:]
    slots = [slots_ref[at] for at in range(5)]
    width = out_ref.shape[1]
    for line in range(out_ref.shape[0]):
        columns = slice(line * width, (line + 1) * width)
        out_ref[line] = grad_rows(piece_refs, ctx_ref, slots, columns)


def call_first_grad(pieces, ctx_blocks, slots):
    width, columns = pieces[0].shape[1] // 4, ctx_blocks.shape[2]
    smem = pl.BlockSpec(memory_space=pltpu.SMEM)
    return pl.pallas_call(
        first_grad,
        out_shape=pltpu.VMEM((4, width, columns), F32),
        in_specs=[smem] + [vmem()] * (len(pieces) + 1),
        out_specs=vmem(),
        compiler_params=params(),
        name="first_grad",
    )(slots, *on_chip(*pieces, ctx_blocks))


def last_grad(slots_ref, core_ref, *refs):
    piece_refs, (ctx_ref, sum_ref, keep_ref, give_ref) = refs[:-4], refs[-4:]
    even_core = core_ref[0] == 0
    slots = [slots_ref[at] for at in range(5, 8)]
    width = sum_ref.shape[1]
    for line in range(sum_ref.shape[0]):
        columns = slice(line * width, (line + 1) * width)
        total = sum_ref[line] + grad_rows(piece_refs, ctx_ref, slots, columns)
        for z in range(8):
            even = total[z * 2 * OWNED : z * 2 * OWNED + OWNED]
            odd = total[z * 2 * OWNED + OWNED : (z + 1) * 2 * OWNED]
            keep_ref[line * 8 + z] = jnp.where(even_core, even, odd)
            give_ref[line * 8 + z] = jnp.where(even_core, odd, even).astype(jnp.bfloat16)


def call_last_grad(pieces, ctx_blocks, sums, slots, core):
    shape = (32, OWNED, ctx_blocks.shape[2])
    smem = pl.BlockSpec(memory_space=pltpu.SMEM)
    return pl.pallas_call(
        last_grad,
        out_shape=(pltpu.VMEM(shape, F32), pltpu.VMEM(shape, jnp.bfloat16)),
        in_specs=[smem, smem] + [vmem()] * (len(pieces) + 2),
        out_specs=(vmem(), vmem()),
        compiler_params=params(),
        name="last_grad",
    )(slots, core, *on_chip(*pieces, ctx_blocks, sums))


def add_pair(keep_ref, given_ref, sum_ref):
    sum_ref[...] = (keep_ref[...] + given_ref[...].astype(F32)).astype(jnp.bfloat16)


def call_add_pair(keep, given):
    return pl.pallas_call(
        add_pair,
        out_shape=pltpu.HBM(given.shape, given.dtype),
        in_specs=[vmem()] * 2,
        out_specs=vmem(),
        compiler_params=params(),
        name="add_pair",
    )(*on_chip(keep, given))


def token_rows(counts, slots_ref, *refs):
    w_ref, out_ref = refs[-2:]
    at = block = 0
    for count in counts:
        rows = jnp.dot(rows_of(refs[at : at + count], slice(None)), w_ref[...], preferred_element_type=F32)
        at += count
        for part in range(rows.shape[0] // 128):
            out_ref[slots_ref[block]] = rows[part * 128 : (part + 1) * 128].astype(jnp.bfloat16)
            block += 1


def call_token_rows(groups, weights, slots):
    columns = weights.shape[1]
    smem = pl.BlockSpec(memory_space=pltpu.SMEM)
    flat = [piece for group in groups for piece in group]
    return pl.pallas_call(
        functools.partial(token_rows, tuple(len(group) for group in groups)),
        out_shape=jax.ShapeDtypeStruct((8, 128, columns), jnp.bfloat16),
        in_specs=[smem] + [vmem()] * (len(flat) + 1),
        out_specs=vmem(),
        compiler_params=params(),
        name="token_rows",
    )(slots, *flat, weights)


def copies_of(count, value_ref, copies_ref):
    for at in range(count):
        copies_ref[at] = value_ref[...].astype(copies_ref.dtype)


def call_copies_of(count, value):
    return pl.pallas_call(
        functools.partial(copies_of, count),
        out_shape=pltpu.HBM((count,) + value.shape, jnp.bfloat16),
        in_specs=[vmem()],
        out_specs=vmem(),
        compiler_params=params(),
    )(*on_chip(value))


def some_rows(begin, value_ref, rows_ref):
    rows_ref[...] = value_ref[begin : begin + rows_ref.shape[0]]


def call_some_rows(value, begin, end):
    return pl.pallas_call(
        functools.partial(some_rows, begin),
        out_shape=pltpu.VMEM((end - begin, value.shape[1]), value.dtype),
        in_specs=[vmem()],
        out_specs=vmem(),
        compiler_params=params(),
    )(*on_chip(value))


def adam(token_count, line_ref, w_ref, m_ref, v_ref, new_w_ref, new_m_ref, new_v_ref, copies_ref):
    total = line_ref[0].astype(F32)
    for at in range(1, line_ref.shape[0]):
        total += line_ref[at].astype(F32)
    grad = total / token_count
    new_first = 0.9 * m_ref[...] + 0.1 * grad
    new_second = 0.95 * v_ref[...] + 0.05 * grad * grad
    first_scale = 1.0 - 0.9**STEP
    second_scale = 1.0 - 0.95**STEP
    update = new_first / first_scale / (jnp.sqrt(new_second / second_scale) + 1e-08)
    new_master = w_ref[...] - 0.001 * update
    new_w_ref[...] = new_master
    new_m_ref[...] = new_first
    new_v_ref[...] = new_second
    rounded = new_master.astype(jnp.bfloat16)
    for at in range(copies_ref.shape[0]):
        copies_ref[at] = rounded


def call_adam(token_count, line, master, first_moment, second_moment):
    state = jax.ShapeDtypeStruct(master.shape, F32)
    return pl.pallas_call(
        functools.partial(adam, float(token_count)),
        out_shape=(state, state, state, pltpu.HBM((32,) + master.shape, jnp.bfloat16)),
        in_specs=[vmem()] * 4,
        out_specs=(vmem(),) * 4,
        compiler_params=params(),
        name="adam",
    )(*on_chip(line, master, first_moment, second_moment))


def interleave(core_ref, mine_ref, other_ref, out_ref):
    even_core = core_ref[0] == 0
    line = pl.program_id(0)
    for z in range(8):
        in_order = len(other_ref.shape) == 3
        mine = mine_ref[z] if in_order else mine_ref[z, line]
        other = other_ref[line * 8 + z] if in_order else other_ref[z, line]
        out_ref[z, 0] = jnp.where(even_core, mine, other)
        out_ref[z, 1] = jnp.where(even_core, other, mine)


def both_cores(mine, core):
    other = shift(mine, "c", 1)
    columns = mine.shape[-1]
    mine_spec = pl.BlockSpec((8, OWNED, columns), lambda line: (line, 0, 0))
    if mine.ndim == 4:
        (mine,), mine_spec = on_chip(mine), vmem()
    out = pl.pallas_call(
        interleave,
        grid=(4,),
        out_shape=jax.ShapeDtypeStruct((32, 2, OWNED, columns), mine.dtype),
        in_specs=[pl.BlockSpec(memory_space=pltpu.SMEM), mine_spec, vmem()],
        out_specs=pl.BlockSpec((8, 2, OWNED, columns), lambda line: (line, 0, 0, 0)),
        compiler_params=params(),
        name="interleave",
    )(core, mine, *on_chip(other))
    return out.reshape(-1, columns)


def exchange(value, axes):
    return lax.all_to_all(value, axes, split_axis=0, concat_axis=0, tiled=True)


def step(cotangent, context, master, first_moment, second_moment):
    core = lax.axis_index("c").astype(jnp.int32).reshape(1)
    x = lax.axis_index("x").astype(jnp.int32)
    yh = lax.axis_index("yh").astype(jnp.int32)
    token_count = context.shape[0] * 64
    columns = context.shape[1]
    ctx_blocks = context.reshape(8, 128, columns)
    offsets = jnp.array([0, 3, 1, 2, 0, 3, 1, 2], jnp.int32)
    flips = jnp.array([0, 0, 0, 0, 1, 1, 1, 1], jnp.int32)
    slots = ((x + offsets) & 3) * 2 + (yh ^ flips)

    partner = shift(cotangent, "yh", 1)
    low, high = shift(cotangent, "x", 1), shift(cotangent, "x", -1)
    far = shift(cotangent, "x", 2)
    low_y, high_y = shift(partner, "x", 1), shift(partner, "x", -1)
    upper = call_some_rows(far, 0, OVER_Y)
    lower = call_some_rows(partner, OVER_Y, partner.shape[0])
    far_a, far_b = shift(upper, "yh", 1), shift(lower, "x", 2)

    line = exchange(call_copies_of(4, master), ("yl",))
    planes = exchange(call_copies_of(8, line), ("z",))
    weights = both_cores(planes, core)

    early = [cotangent, low, high, far, partner]
    sums = call_first_grad(early, ctx_blocks, slots)
    keep, give = call_last_grad([low_y, high_y, far_a, far_b], ctx_blocks, sums, slots, core)
    pair_sum = call_add_pair(keep, shift(give, "c", 1))
    received = exchange(pair_sum, ("yl", "z"))
    new_master, new_first, new_second, copies = call_adam(
        token_count, received, master, first_moment, second_moment
    )
    new_weights = both_cores(exchange(copies, ("yl", "z")), core)
    groups = [[cotangent, low], [high, far], [partner, low_y], [high_y, far_a, far_b]]
    d_context = call_token_rows(groups, weights, slots).reshape(-1, columns)
    return (d_context, new_master, new_first, new_second, new_weights)


def solution(mesh):
    fine = Mesh(mesh.devices.reshape(tuple(SIZES.values())), AXES)
    owner, part = ("yl", "z", "c"), ("x", "yh")
    in_specs = (P(owner + part, None),) + (P(owner, part),) * 4
    out_specs = (P(owner, part),) * 4 + (P(None, part),)
    return jax.shard_map(step, mesh=fine, in_specs=in_specs, out_specs=out_specs, check_vma=False)
```

```python
import functools

import jax
import jax.numpy as jnp
from jax import lax
from jax.experimental import pallas as pl
from jax.experimental.pallas import tpu as pltpu
from jax.sharding import Mesh
from jax.sharding import PartitionSpec as P

STEP = 10
AXES = ("yl", "z", "c", "x", "yh")
SIZES = {"yl": 4, "z": 8, "c": 2, "x": 4, "yh": 2}
OWNED = 48
OVER_Y = 32
F32 = jnp.float32


def shift(value, axis, by):
    count = SIZES[axis]
    return lax.ppermute(value, axis, [(at, (at + by) % count) for at in range(count)])


def vmem():
    return pl.BlockSpec(memory_space=pltpu.VMEM)


def on_chip(*values):
    return [pltpu.with_memory_space_constraint(value, pltpu.VMEM) for value in values]


def params():
    return pltpu.CompilerParams(vmem_limit_bytes=20 * 1024 * 1024)


def rows_of(refs, columns):
    return jnp.concatenate([ref[:, columns] for ref in refs], axis=0)


def grad_rows(refs, ctx_ref, slots, columns):
    ctx = jnp.concatenate([ctx_ref[slot] for slot in slots], axis=0)
    return lax.dot_general(
        rows_of(refs, columns), ctx, (((0,), (0,)), ((), ())), preferred_element_type=F32
    )


def first_grad(slots_ref, *refs):
    piece_refs, (ctx_ref, out_ref) = refs[:-2], refs[-2:]
    slots = [slots_ref[at] for at in range(5)]
    width = out_ref.shape[1]
    for line in range(out_ref.shape[0]):
        columns = slice(line * width, (line + 1) * width)
        out_ref[line] = grad_rows(piece_refs, ctx_ref, slots, columns)


def call_first_grad(pieces, ctx_blocks, slots):
    width, columns = pieces[0].shape[1] // 4, ctx_blocks.shape[2]
    smem = pl.BlockSpec(memory_space=pltpu.SMEM)
    return pl.pallas_call(
        first_grad,
        out_shape=pltpu.VMEM((4, width, columns), F32),
        in_specs=[smem] + [vmem()] * (len(pieces) + 1),
        out_specs=vmem(),
        compiler_params=params(),
        name="first_grad",
    )(slots, *on_chip(*pieces, ctx_blocks))


def last_grad(slots_ref, core_ref, *refs):
    piece_refs, (ctx_ref, sum_ref, keep_ref, give_ref) = refs[:-4], refs[-4:]
    even_core = core_ref[0] == 0
    slots = [slots_ref[at] for at in range(5, 8)]
    width = sum_ref.shape[1]
    for line in range(sum_ref.shape[0]):
        columns = slice(line * width, (line + 1) * width)
        total = sum_ref[line] + grad_rows(piece_refs, ctx_ref, slots, columns)
        for z in range(8):
            even = total[z * 2 * OWNED : z * 2 * OWNED + OWNED]
            odd = total[z * 2 * OWNED + OWNED : (z + 1) * 2 * OWNED]
            keep_ref[line * 8 + z] = jnp.where(even_core, even, odd)
            give_ref[line * 8 + z] = jnp.where(even_core, odd, even).astype(jnp.bfloat16)


def call_last_grad(pieces, ctx_blocks, sums, slots, core):
    shape = (32, OWNED, ctx_blocks.shape[2])
    smem = pl.BlockSpec(memory_space=pltpu.SMEM)
    return pl.pallas_call(
        last_grad,
        out_shape=(pltpu.VMEM(shape, F32), pltpu.VMEM(shape, jnp.bfloat16)),
        in_specs=[smem, smem] + [vmem()] * (len(pieces) + 2),
        out_specs=(vmem(), vmem()),
        compiler_params=params(),
        name="last_grad",
    )(slots, core, *on_chip(*pieces, ctx_blocks, sums))


def add_pair(keep_ref, given_ref, sum_ref):
    sum_ref[...] = (keep_ref[...] + given_ref[...].astype(F32)).astype(jnp.bfloat16)


def call_add_pair(keep, given):
    return pl.pallas_call(
        add_pair,
        out_shape=pltpu.HBM(given.shape, given.dtype),
        in_specs=[vmem()] * 2,
        out_specs=vmem(),
        compiler_params=params(),
        name="add_pair",
    )(*on_chip(keep, given))


def token_rows(counts, slots_ref, *refs):
    w_ref, out_ref = refs[-2:]
    at = block = 0
    for count in counts:
        rows = jnp.dot(rows_of(refs[at : at + count], slice(None)), w_ref[...], preferred_element_type=F32)
        at += count
        for part in range(rows.shape[0] // 128):
            out_ref[slots_ref[block]] = rows[part * 128 : (part + 1) * 128].astype(jnp.bfloat16)
            block += 1


def call_token_rows(groups, weights, slots):
    columns = weights.shape[1]
    smem = pl.BlockSpec(memory_space=pltpu.SMEM)
    flat = [piece for group in groups for piece in group]
    return pl.pallas_call(
        functools.partial(token_rows, tuple(len(group) for group in groups)),
        out_shape=jax.ShapeDtypeStruct((8, 128, columns), jnp.bfloat16),
        in_specs=[smem] + [vmem()] * (len(flat) + 1),
        out_specs=vmem(),
        compiler_params=params(),
        name="token_rows",
    )(slots, *flat, weights)


def copies_of(count, value_ref, copies_ref):
    for at in range(count):
        copies_ref[at] = value_ref[...].astype(copies_ref.dtype)


def call_copies_of(count, value):
    return pl.pallas_call(
        functools.partial(copies_of, count),
        out_shape=pltpu.HBM((count,) + value.shape, jnp.bfloat16),
        in_specs=[vmem()],
        out_specs=vmem(),
        compiler_params=params(),
    )(*on_chip(value))


def some_rows(begin, value_ref, rows_ref):
    rows_ref[...] = value_ref[begin : begin + rows_ref.shape[0]]


def call_some_rows(value, begin, end):
    return pl.pallas_call(
        functools.partial(some_rows, begin),
        out_shape=pltpu.VMEM((end - begin, value.shape[1]), value.dtype),
        in_specs=[vmem()],
        out_specs=vmem(),
        compiler_params=params(),
    )(*on_chip(value))


def adam(token_count, line_ref, w_ref, m_ref, v_ref, new_w_ref, new_m_ref, new_v_ref, copies_ref):
    total = line_ref[0].astype(F32)
    for at in range(1, line_ref.shape[0]):
        total += line_ref[at].astype(F32)
    grad = total / token_count
    new_first = 0.9 * m_ref[...] + 0.1 * grad
    new_second = 0.95 * v_ref[...] + 0.05 * grad * grad
    first_scale = 1.0 - 0.9**STEP
    second_scale = 1.0 - 0.95**STEP
    update = new_first / first_scale / (jnp.sqrt(new_second / second_scale) + 1e-08)
    new_master = w_ref[...] - 0.001 * update
    new_w_ref[...] = new_master
    new_m_ref[...] = new_first
    new_v_ref[...] = new_second
    rounded = new_master.astype(jnp.bfloat16)
    for at in range(copies_ref.shape[0]):
        copies_ref[at] = rounded


def call_adam(token_count, line, master, first_moment, second_moment):
    state = jax.ShapeDtypeStruct(master.shape, F32)
    return pl.pallas_call(
        functools.partial(adam, float(token_count)),
        out_shape=(state, state, state, pltpu.HBM((32,) + master.shape, jnp.bfloat16)),
        in_specs=[vmem()] * 4,
        out_specs=(vmem(),) * 4,
        compiler_params=params(),
        name="adam",
    )(*on_chip(line, master, first_moment, second_moment))


def interleave(core_ref, mine_ref, other_ref, out_ref):
    even_core = core_ref[0] == 0
    line = pl.program_id(0)
    for z in range(8):
        at = (z, line) if len(mine_ref.shape) == 4 else line * 8 + z
        mine, other = mine_ref[at], other_ref[at]
        out_ref[z, 0] = jnp.where(even_core, mine, other)
        out_ref[z, 1] = jnp.where(even_core, other, mine)


def both_cores(mine, core):
    other = shift(mine, "c", 1)
    columns = mine.shape[-1]
    out = pl.pallas_call(
        interleave,
        grid=(4,),
        out_shape=jax.ShapeDtypeStruct((32, 2, OWNED, columns), mine.dtype),
        in_specs=[pl.BlockSpec(memory_space=pltpu.SMEM), vmem(), vmem()],
        out_specs=pl.BlockSpec((8, 2, OWNED, columns), lambda line: (line, 0, 0, 0)),
        compiler_params=params(),
        name="interleave",
    )(core, *on_chip(mine, other))
    return out.reshape(-1, columns)


def exchange(value, axes):
    return lax.all_to_all(value, axes, split_axis=0, concat_axis=0, tiled=True)


def step(cotangent, context, master, first_moment, second_moment):
    core = lax.axis_index("c").astype(jnp.int32).reshape(1)
    x = lax.axis_index("x").astype(jnp.int32)
    yh = lax.axis_index("yh").astype(jnp.int32)
    token_count = context.shape[0] * 64
    columns = context.shape[1]
    ctx_blocks = context.reshape(8, 128, columns)
    offsets = jnp.array([0, 3, 1, 2, 0, 3, 1, 2], jnp.int32)
    flips = jnp.array([0, 0, 0, 0, 1, 1, 1, 1], jnp.int32)
    slots = ((x + offsets) & 3) * 2 + (yh ^ flips)

    partner = shift(cotangent, "yh", 1)
    low, high = shift(cotangent, "x", 1), shift(cotangent, "x", -1)
    far = shift(cotangent, "x", 2)
    low_y, high_y = shift(partner, "x", 1), shift(partner, "x", -1)
    upper = call_some_rows(far, 0, OVER_Y)
    lower = call_some_rows(partner, OVER_Y, partner.shape[0])
    far_a, far_b = shift(upper, "yh", 1), shift(lower, "x", 2)

    line = exchange(call_copies_of(4, master), ("yl",))
    planes = exchange(call_copies_of(8, line), ("z",))
    weights = both_cores(planes, core)

    early = [cotangent, low, high, far, partner]
    sums = call_first_grad(early, ctx_blocks, slots)
    keep, give = call_last_grad([low_y, high_y, far_a, far_b], ctx_blocks, sums, slots, core)
    pair_sum = call_add_pair(keep, shift(give, "c", 1))
    received = exchange(pair_sum, ("yl", "z"))
    new_master, new_first, new_second, copies = call_adam(
        token_count, received, master, first_moment, second_moment
    )
    new_weights = both_cores(exchange(copies, ("yl", "z")), core)
    groups = [[cotangent, low], [high, far], [partner, low_y], [high_y, far_a, far_b]]
    d_context = call_token_rows(groups, weights, slots).reshape(-1, columns)
    return (d_context, new_master, new_first, new_second, new_weights)


def solution(mesh):
    fine = Mesh(mesh.devices.reshape(tuple(SIZES.values())), AXES)
    owner, part = ("yl", "z", "c"), ("x", "yh")
    in_specs = (P(owner + part, None),) + (P(owner, part),) * 4
    out_specs = (P(owner, part),) * 4 + (P(None, part),)
    return jax.shard_map(step, mesh=fine, in_specs=in_specs, out_specs=out_specs, check_vma=False)
```
